32 devices in a mesh: sub: 4 (over x, core), beam: 4 (over z), comp: 2 (over y).
Axes of the slice: x: 2, y: 2, z: 4, core: 2. Of those that a mesh axis runs over, the one named last changes fastest.
Arguments:
- raw_pulses: bfloat16 [4096, 2, 16384], P(('sub', 'beam', 'comp')), may hold values from -6 to 6
- range_filter: float32 [2, 16384], replicated, may hold values from -4 to 4
- steer_angle: float32 [64, 4096], P(None, ('sub', 'beam', 'comp')), may hold values from -3.140625 to 3.140625
- band_offsets: int32 [2, 384], P(None, ('beam', 'comp')), may hold values from -4 to 12, as said below
- band_weights: float32 [2, 384, 8], P(None, ('beam', 'comp')), may hold values from -1.5 to 1.5
- beam_delay: float32 [2, 384], P(None, ('beam', 'comp')), may hold values from -3 to 3
Outputs:
- scene_beams: float32 [256, 2, 16384], P(('beam', 'comp'), None, 'sub')
The draws below stay inside these ranges and needn't reach their ends.
Inputs may be any that keep to these rules, and one draw needn't show every extreme that they name: `band_offsets`: for new beam u of a merge level l and a block (0 <= u < 2 * 8 2^l), each side's offset is u // 2 - 8 // 2 + 1 or one less; the first beam of every level and block takes the lesser value, the last the greater.
All inputs are finite; a program needn't handle non-finite values.
Results may differ from the reference program's by a relative error of at most 0.0059.
Values may be sent and summed in bfloat16 or wider, within the bound.
A program may use at most 128 MiB of HBM per device.

```python
import math
import jax
import jax.numpy as jnp
from jax import lax

NR = 16384
RADIX = 128
NB0 = 8
BAND = 8
PDEV = 128
PSUB = 1024
PULSES = 4096
NBT0 = 64
NEWL = 48
LEVELS = 2
N_SUB = 4
N_BEAM = 4
N_COMP = 2


def draw_band_offsets(key, part):
    blocks = N_BEAM * N_COMP
    centers = []
    first_flags = []
    last_flags = []
    for level_index in range(LEVELS):
        new_beams = 2 * NB0 * 2 ** level_index
        local_beam = jnp.arange(new_beams, dtype=jnp.int32)
        centers.append(local_beam // 2 - BAND // 2 + 1)
        first_flags.append(local_beam == 0)
        last_flags.append(local_beam == new_beams - 1)
    center_row = jnp.concatenate(centers)
    first_row = jnp.concatenate(first_flags)
    last_row = jnp.concatenate(last_flags)
    coin_flip = jax.random.randint(key, (2, blocks, NEWL), 0, 2, dtype=jnp.int32)
    lowered = jnp.where(first_row[None, None, :], 1, jnp.where(last_row[None, None, :], 0, coin_flip))
    return (center_row[None, None, :] - lowered).astype(jnp.int32).reshape(2, blocks * NEWL)


def levels(stream_key, shape, cuts, low, top_value):
    def one(axis_at, blocks):
        heights = jax.random.uniform(jax.random.fold_in(jax.random.fold_in(stream_key, 6), axis_at), (blocks,), jnp.float32, low / len(cuts), top_value / len(cuts))
        return jnp.repeat(jnp.exp(heights), shape[axis_at] // blocks).reshape((-1,) + (1,) * (len(shape) - axis_at - 1))

    loudness = one(*cuts[0])
    for cut in cuts[1:]:
        loudness = loudness * one(*cut)
    return loudness


def centred(key, dims, spread, bound, split=(), kind=jnp.bfloat16):
    drawn = jax.random.normal(key, dims, jnp.float32) * spread
    if len(split) > 0:
        drawn = levels(key, dims, split, -0.22, 0.18) * drawn
    return jnp.clip(drawn, min=-bound, max=bound).astype(kind)


def setup_inputs(seed: int = 0) -> dict:
    key_of = jax.random.split(jax.random.key(seed), 7)
    raw_pulses = centred(key_of[0], (PULSES, 2, NR), 1.0, 6.0, ((0, 32),))
    range_filter = centred(key_of[1], (2, NR), 0.7071, 4.0, (), jnp.float32)
    steer_angle = jnp.clip(jax.random.uniform(key_of[2], (NBT0, PULSES), jnp.float32, -3.140625, 3.140625), -3.140625, 3.140625)
    band_offsets = draw_band_offsets(jax.random.fold_in(key_of[6], 71), 0)
    band_weights = centred(key_of[4], (2, NEWL * N_BEAM * N_COMP, BAND), 0.25, 1.5, ((1, 8),), jnp.float32)
    beam_delay = jnp.clip(jax.random.uniform(key_of[5], (2, NEWL * N_BEAM * N_COMP), jnp.float32, -3.0, 3.0) * levels(key_of[5], (2, NEWL * N_BEAM * N_COMP), ((1, 8),), -0.4, 0.0), -3.0, 3.0)
    return dict(raw_pulses=raw_pulses, range_filter=range_filter, steer_angle=steer_angle, band_offsets=band_offsets, band_weights=band_weights, beam_delay=beam_delay)


def dft_table(length):
    index_row = jnp.arange(length, dtype=jnp.int32)
    product = (index_row[:, None] * index_row[None, :]) % length
    phase_angle = product.astype(jnp.float32) * (2.0 * math.pi / length)
    return jnp.cos(phase_angle).astype(jnp.bfloat16), (-jnp.sin(phase_angle)).astype(jnp.bfloat16)


def real_form(length):
    cos_part, sin_part = dft_table(length)
    upper_rows = jnp.concatenate([cos_part, sin_part], axis=1)
    lower_rows = jnp.concatenate([-sin_part, cos_part], axis=1)
    return jnp.concatenate([upper_rows, lower_rows], axis=0)


def twiddle():
    freq_index = jnp.arange(RADIX, dtype=jnp.int32)[:, None]
    time_index = jnp.arange(RADIX, dtype=jnp.int32)[None, :]
    phase_angle = ((freq_index * time_index) % NR).astype(jnp.float32) * (2.0 * math.pi / NR)
    return jnp.cos(phase_angle), -jnp.sin(phase_angle)


def compress(raw, range_filter):
    number = raw.shape[0]
    samples = raw.reshape(number, 2 * RADIX, RADIX).astype(jnp.float32)
    first_form = real_form(RADIX).astype(jnp.float32)
    section_one = jnp.einsum('pan,ak->pkn', samples, first_form, precision=lax.Precision.HIGHEST)
    cos_part, sin_part = twiddle()
    real_in = section_one[:, :RADIX]
    imag_in = section_one[:, RADIX:]
    turned = jnp.stack([real_in * cos_part - imag_in * sin_part, real_in * sin_part + imag_in * cos_part], 1)
    turned = turned.astype(jnp.bfloat16).astype(jnp.float32)
    second = real_form(RADIX).reshape(2, RADIX, 2, RADIX).astype(jnp.float32)
    spectrum = jnp.einsum('prkn,rnsm->psmk', turned, second, precision=lax.Precision.HIGHEST)
    spectrum = spectrum.reshape(number, 2, NR)
    factor = NR ** -0.5
    real_out = (spectrum[:, 0] * range_filter[0] - spectrum[:, 1] * range_filter[1]) * factor
    imag_out = (spectrum[:, 0] * range_filter[1] + spectrum[:, 1] * range_filter[0]) * factor
    return jnp.stack([real_out, imag_out], 1).astype(jnp.bfloat16)


def steering(phase_angle, factor):
    real_part = (jnp.cos(phase_angle) * factor).astype(jnp.bfloat16)
    imag_part = (jnp.sin(phase_angle) * factor).astype(jnp.bfloat16)
    return jnp.stack([jnp.stack([real_part, -imag_part], -1), jnp.stack([imag_part, real_part], -1)], 1)


def beam_term(weights, pulses):
    return jnp.einsum('kspq,pqr->ksr', weights.astype(jnp.float32), pulses.astype(jnp.float32),
                      precision=lax.Precision.HIGHEST)


def band_matrix(offset, weight, span):
    tap_index = offset[:, None] + BAND // 2 + jnp.arange(BAND, dtype=jnp.int32)[None, :]
    matches = tap_index[:, :, None] == jnp.arange(span, dtype=jnp.int32)[None, None, :]
    return jnp.sum(jnp.where(matches, weight[:, :, None], jnp.zeros_like(weight)[:, :, None]), axis=1)


def merge_level(subimage, level_index, band_offsets, band_weights, beam_delay):
    blocks = N_BEAM * N_COMP
    old_beams = NB0 * 2 ** level_index
    new_beams = 2 * old_beams
    column_base = NB0 * (2 ** (level_index + 1) - 2)
    margin = BAND // 2
    groups = subimage.shape[0] // 2
    padded = jnp.pad(subimage, ((0, 0), (margin, margin), (0, 0), (0, 0)))
    paired = padded.reshape(groups, 2, padded.shape[1], 2, NR)
    range_rows = jnp.arange(NR, dtype=jnp.int32).astype(jnp.float32)
    pieces = []
    for block in range(blocks):
        window = paired[:, :, block * old_beams: block * old_beams + old_beams + 2 * margin]
        col_start = block * NEWL + column_base
        real_sum = jnp.zeros((groups, new_beams, NR), jnp.float32)
        imag_sum = jnp.zeros((groups, new_beams, NR), jnp.float32)
        for parity in range(2):
            matrix = band_matrix(band_offsets[parity, col_start:col_start + new_beams],
                                 band_weights[parity, col_start:col_start + new_beams], old_beams + 2 * margin)
            blended = jnp.einsum('jw,gwsr->gjsr', matrix, window[:, parity], precision=lax.Precision.HIGHEST)
            phase_angle = beam_delay[parity, col_start:col_start + new_beams][:, None] * (1.0 + range_rows / NR)[None, :]
            cosine = jnp.cos(phase_angle)
            sine_part = jnp.sin(phase_angle)
            real_sum = real_sum + (cosine * blended[:, :, 0] - sine_part * blended[:, :, 1])
            imag_sum = imag_sum + (sine_part * blended[:, :, 0] + cosine * blended[:, :, 1])
        pieces.append(jnp.stack([real_sum, imag_sum], 2))
    return jnp.concatenate(pieces, 1)


def reference(raw_pulses, range_filter, steer_angle, band_offsets, band_weights, beam_delay):
    blocks = N_BEAM * N_COMP
    runs = raw_pulses.reshape(N_SUB, blocks, PDEV, 2, NR)
    angles = steer_angle.reshape(NBT0, N_SUB, blocks, PDEV).transpose(1, 2, 0, 3)
    factor = float(PSUB) ** -0.5

    def subaperture(sub_item):
        def add_run(summed, run_item):
            pulses = compress(run_item[0], range_filter)
            weights = steering(run_item[1], factor)
            return summed + beam_term(weights, pulses), None

        summed, _ = lax.scan(add_run, jnp.zeros((NBT0, 2, NR), jnp.float32), sub_item)
        return summed

    subimage = lax.map(subaperture, (runs, angles))
    for level_index in range(LEVELS):
        subimage = merge_level(subimage, level_index, band_offsets, band_weights, beam_delay)
    return subimage[0]
```

```python
import math

import jax
import jax.numpy as jnp
from jax import lax
from jax.sharding import PartitionSpec as P

NR = 16384
RADIX = 128
BAND = 8


def from_partner(block, axis, bit):
    count = lax.axis_size(axis)
    route = []
    for low in range(count):
        high = low | 1 << bit
        if high != low and high < count:
            route += [(low, high), (high, low)]
    return lax.ppermute(block, axis, route)


def with_halo(block, sides, width):
    for axis, dim in sides:
        count = lax.axis_size(axis)
        forward = [(i, i + 1) for i in range(count - 1)]
        backward = [(target, source) for source, target in forward]
        low = lax.ppermute(
            lax.slice_in_dim(block, block.shape[dim] - width, None, axis=dim), axis, forward
        )
        high = lax.ppermute(lax.slice_in_dim(block, 0, width, axis=dim), axis, backward)
        block = jnp.concatenate([low, block, high], axis=dim)
    return block


def dft_table(length):
    index_row = jnp.arange(length, dtype=jnp.int32)
    product = index_row[:, None] * index_row[None, :] % length
    phase_angle = product.astype(jnp.float32) * (2.0 * math.pi / length)
    return (jnp.cos(phase_angle).astype(jnp.bfloat16), (-jnp.sin(phase_angle)).astype(jnp.bfloat16))


def real_form(length):
    cos_part, sin_part = dft_table(length)
    upper_rows = jnp.concatenate([cos_part, sin_part], axis=1)
    lower_rows = jnp.concatenate([-sin_part, cos_part], axis=1)
    return jnp.concatenate([upper_rows, lower_rows], axis=0)


def twiddle():
    freq_index = jnp.arange(RADIX, dtype=jnp.int32)[:, None]
    time_index = jnp.arange(RADIX, dtype=jnp.int32)[None, :]
    phase_angle = (freq_index * time_index % NR).astype(jnp.float32) * (2.0 * math.pi / NR)
    return (jnp.cos(phase_angle), -jnp.sin(phase_angle))


def compress(beams, range_filter):
    number = beams.shape[0]
    samples = beams.reshape(number, 2 * RADIX, RADIX)
    section_one = jnp.einsum(
        "pan,ak->pkn", samples, real_form(RADIX), preferred_element_type=jnp.float32
    )
    cos_part, sin_part = twiddle()
    real_in = section_one[:, :RADIX]
    imag_in = section_one[:, RADIX:]
    turned = jnp.stack(
        [real_in * cos_part - imag_in * sin_part, real_in * sin_part + imag_in * cos_part], 1
    )
    second = real_form(RADIX).reshape(2, RADIX, 2, RADIX)
    high = turned.astype(jnp.bfloat16)
    low = (turned - high.astype(jnp.float32)).astype(jnp.bfloat16)
    spectrum = jnp.einsum("prkn,rnsm->psmk", high, second, preferred_element_type=jnp.float32)
    spectrum += jnp.einsum("prkn,rnsm->psmk", low, second, preferred_element_type=jnp.float32)
    spectrum = spectrum.reshape(number, 2, NR)
    factor = NR ** (-0.5)
    real_out = (spectrum[:, 0] * range_filter[0] - spectrum[:, 1] * range_filter[1]) * factor
    imag_out = (spectrum[:, 0] * range_filter[1] + spectrum[:, 1] * range_filter[0]) * factor
    return jnp.stack([real_out, imag_out], 1)


def steering(phase_angle, factor):
    real_part = (jnp.cos(phase_angle) * factor).astype(jnp.bfloat16)
    imag_part = (jnp.sin(phase_angle) * factor).astype(jnp.bfloat16)
    return jnp.stack(
        [jnp.stack([real_part, -imag_part], -1), jnp.stack([imag_part, real_part], -1)], 1
    )


def beam_term(weights, pulses):
    return jnp.einsum("kspq,pqr->ksr", weights, pulses, preferred_element_type=jnp.float32)


def band_matrix(offset, weight, span):
    tap_index = offset[:, None] + BAND // 2 + jnp.arange(BAND, dtype=jnp.int32)[None, :]
    matches = tap_index[:, :, None] == jnp.arange(span, dtype=jnp.int32)[None, None, :]
    return jnp.sum(
        jnp.where(matches, weight[:, :, None], jnp.zeros_like(weight)[:, :, None]), axis=1
    )


def contribute(window, offset, weight, delay_row, range_rows):
    span = window.shape[0]
    matrix = band_matrix(offset, weight, span)
    blended = jnp.dot(
        matrix,
        window.reshape(span, -1).astype(jnp.float32),
        precision=lax.Precision.HIGHEST,
        preferred_element_type=jnp.float32,
    )
    blended = blended.reshape(offset.shape[0], 2, range_rows.shape[0], range_rows.shape[1])
    phase_angle = delay_row[:, None, None] * (1.0 + range_rows / NR)[None]
    cosine = jnp.cos(phase_angle)
    sine_part = jnp.sin(phase_angle)
    return (
        cosine * blended[:, 0] - sine_part * blended[:, 1],
        sine_part * blended[:, 0] + cosine * blended[:, 1],
    )


def body(raw_pulses, range_filter, steer_angle, band_offsets, band_weights, beam_delay):
    beam_devices = lax.axis_size("beam")
    comp_devices = lax.axis_size("comp")
    blocks = beam_devices * comp_devices
    pulses_sub = raw_pulses.shape[0] * blocks
    factor = float(pulses_sub) ** (-0.5)
    first_beams = steer_angle.shape[0] // blocks
    weights = steering(steer_angle, factor)
    sub_count = lax.axis_size("sub")
    levels = sub_count.bit_length() - 1
    sub_index = lax.axis_index("sub")
    partial = beam_term(weights, raw_pulses).astype(jnp.bfloat16)
    summed = lax.psum_scatter(partial, ("beam", "comp"), scatter_dimension=0, tiled=True)
    subimage = compress(summed, range_filter)
    margin = BAND // 2
    block_rows = NR // sub_count
    beam_count = first_beams
    subimage = subimage.reshape(beam_count, 2, sub_count, block_rows)
    for level_index in range(levels):
        kept_blocks = subimage.shape[2] // 2
        parity = sub_index >> level_index & 1
        low_bits = sub_index & (1 << level_index) - 1
        halves = subimage.astype(jnp.bfloat16).reshape(beam_count, 2, kept_blocks, 2, block_rows)
        own_plain = lax.dynamic_index_in_dim(halves, parity, 3, keepdims=False)
        for_peer = lax.dynamic_index_in_dim(halves, 1 - parity, 3, keepdims=False)
        peer_plain = from_partner(for_peer, "sub", level_index)
        children = with_halo(
            jnp.stack([own_plain, peer_plain], 1), ((("beam", "comp"), 0),), margin
        )
        own_child = children[:, 0]
        peer_child = children[:, 1]
        new_beams = 2 * beam_count
        column_base = first_beams * (2 ** (level_index + 1) - 2)
        level_offsets = band_offsets[:, column_base : column_base + new_beams]
        level_weights = band_weights[:, column_base : column_base + new_beams]
        level_delays = beam_delay[:, column_base : column_base + new_beams]
        block_ids = jnp.arange(kept_blocks, dtype=jnp.int32)
        block_starts = (
            block_ids << level_index + 1 | parity << level_index | low_bits
        ) * block_rows
        range_rows = (
            block_starts[:, None] + jnp.arange(block_rows, dtype=jnp.int32)[None, :]
        ).astype(jnp.float32)
        real_own, imag_own = contribute(
            own_child,
            lax.dynamic_index_in_dim(level_offsets, parity, 0, keepdims=False),
            lax.dynamic_index_in_dim(level_weights, parity, 0, keepdims=False),
            lax.dynamic_index_in_dim(level_delays, parity, 0, keepdims=False),
            range_rows,
        )
        real_peer, imag_peer = contribute(
            peer_child,
            lax.dynamic_index_in_dim(level_offsets, 1 - parity, 0, keepdims=False),
            lax.dynamic_index_in_dim(level_weights, 1 - parity, 0, keepdims=False),
            lax.dynamic_index_in_dim(level_delays, 1 - parity, 0, keepdims=False),
            range_rows,
        )
        subimage = jnp.stack([real_own + real_peer, imag_own + imag_peer], 1)
        beam_count = new_beams
    return subimage.reshape(beam_count, 2, block_rows)


def solution(mesh):
    in_specs = (
        P(("sub", "beam", "comp"), None, None),
        P(),
        P(None, ("sub", "beam", "comp")),
        P(None, ("beam", "comp")),
        P(None, ("beam", "comp"), None),
        P(None, ("beam", "comp")),
    )
    out_specs = P(("beam", "comp"), None, "sub")
    return jax.shard_map(body, mesh=mesh, in_specs=in_specs, out_specs=out_specs, check_vma=False)
```

```python
import functools
import math

import jax
import jax.numpy as jnp
from jax import lax
from jax.experimental import pallas as pl
from jax.experimental.pallas import tpu as pltpu
from jax.sharding import PartitionSpec as P

NR = 16384
RADIX = 128
BAND = 8
CHUNKS = 8
MESH = pl.DeviceIdType.MESH


def from_partner(block, axis, bit):
    count = lax.axis_size(axis)
    route = []
    for low in range(count):
        high = low | 1 << bit
        if high != low and high < count:
            route += [(low, high), (high, low)]
    return lax.ppermute(block, axis, route)


def with_halo(block, sides, width):
    for axis, dim in sides:
        count = lax.axis_size(axis)
        forward = [(i, i + 1) for i in range(count - 1)]
        backward = [(target, source) for source, target in forward]
        low = lax.ppermute(
            lax.slice_in_dim(block, block.shape[dim] - width, None, axis=dim), axis, forward
        )
        high = lax.ppermute(lax.slice_in_dim(block, 0, width, axis=dim), axis, backward)
        block = jnp.concatenate([low, block, high], axis=dim)
    return block


def dft_table(length):
    index_row = jnp.arange(length, dtype=jnp.int32)
    product = index_row[:, None] * index_row[None, :] % length
    phase_angle = product.astype(jnp.float32) * (2.0 * math.pi / length)
    return (jnp.cos(phase_angle).astype(jnp.bfloat16), (-jnp.sin(phase_angle)).astype(jnp.bfloat16))


def real_form(length):
    cos_part, sin_part = dft_table(length)
    upper_rows = jnp.concatenate([cos_part, sin_part], axis=1)
    lower_rows = jnp.concatenate([-sin_part, cos_part], axis=1)
    return jnp.concatenate([upper_rows, lower_rows], axis=0)


def twiddle():
    freq_index = jnp.arange(RADIX, dtype=jnp.int32)[:, None]
    time_index = jnp.arange(RADIX, dtype=jnp.int32)[None, :]
    phase_angle = (freq_index * time_index % NR).astype(jnp.float32) * (2.0 * math.pi / NR)
    return (jnp.cos(phase_angle), -jnp.sin(phase_angle))


def compress(beams, range_filter):
    number = beams.shape[0]
    samples = beams.reshape(number, 2 * RADIX, RADIX)
    section_one = jnp.einsum(
        "pan,ak->pkn", samples, real_form(RADIX), preferred_element_type=jnp.float32
    )
    cos_part, sin_part = twiddle()
    real_in = section_one[:, :RADIX]
    imag_in = section_one[:, RADIX:]
    turned = jnp.stack(
        [real_in * cos_part - imag_in * sin_part, real_in * sin_part + imag_in * cos_part], 1
    )
    second = real_form(RADIX).reshape(2, RADIX, 2, RADIX)
    high = turned.astype(jnp.bfloat16)
    low = (turned - high.astype(jnp.float32)).astype(jnp.bfloat16)
    spectrum = jnp.einsum("prkn,rnsm->psmk", high, second, preferred_element_type=jnp.float32)
    spectrum += jnp.einsum("prkn,rnsm->psmk", low, second, preferred_element_type=jnp.float32)
    spectrum = spectrum.reshape(number, 2, NR)
    factor = NR ** (-0.5)
    real_out = (spectrum[:, 0] * range_filter[0] - spectrum[:, 1] * range_filter[1]) * factor
    imag_out = (spectrum[:, 0] * range_filter[1] + spectrum[:, 1] * range_filter[0]) * factor
    return jnp.stack([real_out, imag_out], 1)


def steering(phase_angle, factor):
    real_part = (jnp.cos(phase_angle) * factor).astype(jnp.bfloat16)
    imag_part = (jnp.sin(phase_angle) * factor).astype(jnp.bfloat16)
    return jnp.stack(
        [jnp.stack([real_part, -imag_part], -1), jnp.stack([imag_part, real_part], -1)], 1
    )


def beam_term(weights, pulses):
    return jnp.einsum("kspq,pqr->ksr", weights, pulses, preferred_element_type=jnp.float32)


def reduce_kernel(
    beam_count, comp_count, part_ref, out_ref, recv_one, send_two, recv_two,
    one_send, one_recv, two_send, two_recv,
):
    z = lax.axis_index("beam")
    y = lax.axis_index("comp")
    width = part_ref.shape[-1] // CHUNKS
    barrier = pltpu.get_barrier_semaphore()
    for d in range(1, comp_count):
        pl.semaphore_signal(
            barrier, inc=1, device_id={"comp": lax.rem(y + d, comp_count)}, device_id_type=MESH
        )
    for d in range(1, beam_count):
        pl.semaphore_signal(
            barrier, inc=1, device_id={"beam": lax.rem(z + d, beam_count)}, device_id_type=MESH
        )
    pl.semaphore_wait(barrier, comp_count + beam_count - 2)
    first = []
    for j in range(CHUNKS):
        cols = pl.ds(j * width, width)
        for d in range(1, comp_count):
            peer = lax.rem(y + d, comp_count)
            copy = pltpu.make_async_remote_copy(
                src_ref=part_ref.at[:, peer, :, cols],
                dst_ref=recv_one.at[d - 1, :, :, cols],
                send_sem=one_send.at[d - 1, j],
                recv_sem=one_recv.at[d - 1, j],
                device_id={"comp": peer},
                device_id_type=MESH,
            )
            copy.start()
            first.append(copy)
    second = []
    for j in range(CHUNKS):
        cols = pl.ds(j * width, width)
        for copy in first[j * (comp_count - 1) : (j + 1) * (comp_count - 1)]:
            copy.wait_recv()
        total = part_ref[:, y, :, cols].astype(jnp.float32)
        for d in range(1, comp_count):
            total += recv_one[d - 1, :, :, cols].astype(jnp.float32)
        send_two[:, :, cols] = total.astype(jnp.bfloat16)
        for d in range(1, beam_count):
            peer = lax.rem(z + d, beam_count)
            copy = pltpu.make_async_remote_copy(
                src_ref=send_two.at[peer, :, cols],
                dst_ref=recv_two.at[d - 1, :, cols],
                send_sem=two_send.at[d - 1, j],
                recv_sem=two_recv.at[d - 1, j],
                device_id={"beam": peer},
                device_id_type=MESH,
            )
            copy.start()
            second.append(copy)
    for j in range(CHUNKS):
        cols = pl.ds(j * width, width)
        for copy in second[j * (beam_count - 1) : (j + 1) * (beam_count - 1)]:
            copy.wait_recv()
        total = part_ref[z, y, :, cols].astype(jnp.float32)
        for d in range(1, comp_count):
            total += recv_one[d - 1, z, :, cols].astype(jnp.float32)
        for d in range(1, beam_count):
            total += recv_two[d - 1, :, cols].astype(jnp.float32)
        out_ref[:, cols] = total
    for copy in first + second:
        copy.wait_send()


def reduce_beams(partial, beam_count, comp_count):
    blocks = beam_count * comp_count
    rows = partial.shape[0] // blocks
    length = partial.size // partial.shape[0]
    part = partial.reshape(beam_count, comp_count, rows, length)
    return pl.pallas_call(
        functools.partial(reduce_kernel, beam_count, comp_count),
        out_shape=jax.ShapeDtypeStruct((rows, length), jnp.float32),
        in_specs=[pl.BlockSpec(memory_space=pltpu.VMEM)],
        out_specs=pl.BlockSpec(memory_space=pltpu.VMEM),
        scratch_shapes=[
            pltpu.VMEM((comp_count - 1, beam_count, rows, length), jnp.bfloat16),
            pltpu.VMEM((beam_count, rows, length), jnp.bfloat16),
            pltpu.VMEM((beam_count - 1, rows, length), jnp.bfloat16),
            pltpu.SemaphoreType.DMA((comp_count - 1, CHUNKS)),
            pltpu.SemaphoreType.DMA((comp_count - 1, CHUNKS)),
            pltpu.SemaphoreType.DMA((beam_count - 1, CHUNKS)),
            pltpu.SemaphoreType.DMA((beam_count - 1, CHUNKS)),
        ],
        compiler_params=pltpu.CompilerParams(
            collective_id=0, has_side_effects=True, vmem_limit_bytes=56 * 2**20
        ),
    )(part)


def band_matrix(offset, weight, span):
    tap_index = offset[:, None] + BAND // 2 + jnp.arange(BAND, dtype=jnp.int32)[None, :]
    matches = tap_index[:, :, None] == jnp.arange(span, dtype=jnp.int32)[None, None, :]
    return jnp.sum(
        jnp.where(matches, weight[:, :, None], jnp.zeros_like(weight)[:, :, None]), axis=1
    )


def contribute(window, offset, weight, delay_row, range_rows):
    span = window.shape[0]
    matrix = band_matrix(offset, weight, span)
    blended = jnp.dot(
        matrix,
        window.reshape(span, -1).astype(jnp.float32),
        precision=lax.Precision.HIGHEST,
        preferred_element_type=jnp.float32,
    )
    blended = blended.reshape(offset.shape[0], 2, range_rows.shape[0], range_rows.shape[1])
    phase_angle = delay_row[:, None, None] * (1.0 + range_rows / NR)[None]
    cosine = jnp.cos(phase_angle)
    sine_part = jnp.sin(phase_angle)
    return (
        cosine * blended[:, 0] - sine_part * blended[:, 1],
        sine_part * blended[:, 0] + cosine * blended[:, 1],
    )


def body(raw_pulses, range_filter, steer_angle, band_offsets, band_weights, beam_delay):
    beam_devices = lax.axis_size("beam")
    comp_devices = lax.axis_size("comp")
    blocks = beam_devices * comp_devices
    pulses_sub = raw_pulses.shape[0] * blocks
    factor = float(pulses_sub) ** (-0.5)
    first_beams = steer_angle.shape[0] // blocks
    weights = steering(steer_angle, factor)
    sub_count = lax.axis_size("sub")
    levels = sub_count.bit_length() - 1
    sub_index = lax.axis_index("sub")
    partial = beam_term(weights, raw_pulses).astype(jnp.bfloat16)
    summed = reduce_beams(partial, beam_devices, comp_devices)
    subimage = compress(summed.astype(jnp.bfloat16), range_filter)
    margin = BAND // 2
    block_rows = NR // sub_count
    beam_count = first_beams
    subimage = subimage.reshape(beam_count, 2, sub_count, block_rows)
    for level_index in range(levels):
        kept_blocks = subimage.shape[2] // 2
        parity = sub_index >> level_index & 1
        low_bits = sub_index & (1 << level_index) - 1
        halves = subimage.astype(jnp.bfloat16).reshape(beam_count, 2, kept_blocks, 2, block_rows)
        own_plain = lax.dynamic_index_in_dim(halves, parity, 3, keepdims=False)
        for_peer = lax.dynamic_index_in_dim(halves, 1 - parity, 3, keepdims=False)
        peer_plain = from_partner(for_peer, "sub", level_index)
        children = with_halo(
            jnp.stack([own_plain, peer_plain], 1), ((("beam", "comp"), 0),), margin
        )
        own_child = children[:, 0]
        peer_child = children[:, 1]
        new_beams = 2 * beam_count
        column_base = first_beams * (2 ** (level_index + 1) - 2)
        level_offsets = band_offsets[:, column_base : column_base + new_beams]
        level_weights = band_weights[:, column_base : column_base + new_beams]
        level_delays = beam_delay[:, column_base : column_base + new_beams]
        block_ids = jnp.arange(kept_blocks, dtype=jnp.int32)
        block_starts = (
            block_ids << level_index + 1 | parity << level_index | low_bits
        ) * block_rows
        range_rows = (
            block_starts[:, None] + jnp.arange(block_rows, dtype=jnp.int32)[None, :]
        ).astype(jnp.float32)
        real_own, imag_own = contribute(
            own_child,
            lax.dynamic_index_in_dim(level_offsets, parity, 0, keepdims=False),
            lax.dynamic_index_in_dim(level_weights, parity, 0, keepdims=False),
            lax.dynamic_index_in_dim(level_delays, parity, 0, keepdims=False),
            range_rows,
        )
        real_peer, imag_peer = contribute(
            peer_child,
            lax.dynamic_index_in_dim(level_offsets, 1 - parity, 0, keepdims=False),
            lax.dynamic_index_in_dim(level_weights, 1 - parity, 0, keepdims=False),
            lax.dynamic_index_in_dim(level_delays, 1 - parity, 0, keepdims=False),
            range_rows,
        )
        subimage = jnp.stack([real_own + real_peer, imag_own + imag_peer], 1)
        beam_count = new_beams
    return subimage.reshape(beam_count, 2, block_rows)


def solution(mesh):
    in_specs = (
        P(("sub", "beam", "comp"), None, None),
        P(),
        P(None, ("sub", "beam", "comp")),
        P(None, ("beam", "comp")),
        P(None, ("beam", "comp"), None),
        P(None, ("beam", "comp")),
    )
    out_specs = P(("beam", "comp"), None, "sub")
    return jax.shard_map(body, mesh=mesh, in_specs=in_specs, out_specs=out_specs, check_vma=False)
```

```python
import functools
import math

import jax
import jax.numpy as jnp
from jax import lax
from jax.experimental import pallas as pl
from jax.experimental.pallas import tpu as pltpu
from jax.sharding import PartitionSpec as P

NR = 16384
RADIX = 128
BAND = 8
CHUNKS = 8
MESH = pl.DeviceIdType.MESH


def dft_table(length):
    index_row = jnp.arange(length, dtype=jnp.int32)
    product = index_row[:, None] * index_row[None, :] % length
    phase_angle = product.astype(jnp.float32) * (2.0 * math.pi / length)
    return (jnp.cos(phase_angle).astype(jnp.bfloat16), (-jnp.sin(phase_angle)).astype(jnp.bfloat16))


def real_form(length):
    cos_part, sin_part = dft_table(length)
    upper_rows = jnp.concatenate([cos_part, sin_part], axis=1)
    lower_rows = jnp.concatenate([-sin_part, cos_part], axis=1)
    return jnp.concatenate([upper_rows, lower_rows], axis=0)


def twiddle():
    freq_index = jnp.arange(RADIX, dtype=jnp.int32)[:, None]
    time_index = jnp.arange(RADIX, dtype=jnp.int32)[None, :]
    phase_angle = (freq_index * time_index % NR).astype(jnp.float32) * (2.0 * math.pi / NR)
    return (jnp.cos(phase_angle), -jnp.sin(phase_angle))


def compress(beams, range_filter):
    number = beams.shape[1]
    samples = beams.reshape(2, number, RADIX, RADIX)
    first = real_form(RADIX).reshape(2, RADIX, 2, RADIX)
    section_one = jnp.einsum("rpan,rask->spkn", samples, first, preferred_element_type=jnp.float32)
    cos_part, sin_part = twiddle()
    real_in = section_one[0]
    imag_in = section_one[1]
    turned = jnp.stack(
        [real_in * cos_part - imag_in * sin_part, real_in * sin_part + imag_in * cos_part], 0
    )
    high = turned.astype(jnp.bfloat16)
    low = (turned - high.astype(jnp.float32)).astype(jnp.bfloat16)
    spectrum = jnp.einsum("rpkn,rnsm->spmk", high, first, preferred_element_type=jnp.float32)
    spectrum += jnp.einsum("rpkn,rnsm->spmk", low, first, preferred_element_type=jnp.float32)
    spectrum = spectrum.reshape(2, number, NR)
    factor = NR ** (-0.5)
    real_out = (spectrum[0] * range_filter[0] - spectrum[1] * range_filter[1]) * factor
    imag_out = (spectrum[0] * range_filter[1] + spectrum[1] * range_filter[0]) * factor
    return jnp.stack([real_out, imag_out], 0)


def steering(phase_angle, factor):
    real_part = (jnp.cos(phase_angle) * factor).astype(jnp.bfloat16)
    imag_part = (jnp.sin(phase_angle) * factor).astype(jnp.bfloat16)
    return jnp.stack(
        [jnp.stack([real_part, -imag_part], -1), jnp.stack([imag_part, real_part], -1)], 1
    )


def beam_term(weights, pulses):
    return jnp.einsum("kspq,pqr->skr", weights, pulses, preferred_element_type=jnp.float32)


def reduce_kernel(
    beam_count, comp_count, part_ref, out_ref, recv_one, send_two, recv_two,
    one_send, one_recv, two_send, two_recv,
):
    z = lax.axis_index("beam")
    y = lax.axis_index("comp")
    width = part_ref.shape[-1] // CHUNKS
    barrier = pltpu.get_barrier_semaphore()
    for d in range(1, comp_count):
        pl.semaphore_signal(
            barrier, inc=1, device_id={"comp": lax.rem(y + d, comp_count)}, device_id_type=MESH
        )
    for d in range(1, beam_count):
        pl.semaphore_signal(
            barrier, inc=1, device_id={"beam": lax.rem(z + d, beam_count)}, device_id_type=MESH
        )
    pl.semaphore_wait(barrier, comp_count + beam_count - 2)
    first = []
    for j in range(CHUNKS):
        cols = pl.ds(j * width, width)
        for d in range(1, comp_count):
            peer = lax.rem(y + d, comp_count)
            copy = pltpu.make_async_remote_copy(
                src_ref=part_ref.at[:, :, peer, :, cols],
                dst_ref=recv_one.at[d - 1, :, :, :, cols],
                send_sem=one_send.at[d - 1, j],
                recv_sem=one_recv.at[d - 1, j],
                device_id={"comp": peer},
                device_id_type=MESH,
            )
            copy.start()
            first.append(copy)
    second = []
    for j in range(CHUNKS):
        cols = pl.ds(j * width, width)
        for copy in first[j * (comp_count - 1) : (j + 1) * (comp_count - 1)]:
            copy.wait_recv()
        total = part_ref[:, :, y, :, cols].astype(jnp.float32)
        for d in range(1, comp_count):
            total += recv_one[d - 1, :, :, :, cols].astype(jnp.float32)
        send_two[:, :, :, cols] = total.astype(jnp.bfloat16)
        for d in range(1, beam_count):
            peer = lax.rem(z + d, beam_count)
            copy = pltpu.make_async_remote_copy(
                src_ref=send_two.at[:, peer, :, cols],
                dst_ref=recv_two.at[d - 1, :, :, cols],
                send_sem=two_send.at[d - 1, j],
                recv_sem=two_recv.at[d - 1, j],
                device_id={"beam": peer},
                device_id_type=MESH,
            )
            copy.start()
            second.append(copy)
    for j in range(CHUNKS):
        cols = pl.ds(j * width, width)
        for copy in second[j * (beam_count - 1) : (j + 1) * (beam_count - 1)]:
            copy.wait_recv()
        total = part_ref[:, z, y, :, cols].astype(jnp.float32)
        for d in range(1, comp_count):
            total += recv_one[d - 1, :, z, :, cols].astype(jnp.float32)
        for d in range(1, beam_count):
            total += recv_two[d - 1, :, :, cols].astype(jnp.float32)
        out_ref[:, :, cols] = total.astype(jnp.bfloat16)
    for copy in first + second:
        copy.wait_send()


def reduce_beams(partial, beam_count, comp_count):
    blocks = beam_count * comp_count
    rows = partial.shape[1] // blocks
    length = partial.shape[2]
    part = partial.reshape(2, beam_count, comp_count, rows, length)
    return pl.pallas_call(
        functools.partial(reduce_kernel, beam_count, comp_count),
        out_shape=jax.ShapeDtypeStruct((2, rows, length), jnp.bfloat16),
        in_specs=[pl.BlockSpec(memory_space=pltpu.VMEM)],
        out_specs=pl.BlockSpec(memory_space=pltpu.VMEM),
        scratch_shapes=[
            pltpu.VMEM((comp_count - 1, 2, beam_count, rows, length), jnp.bfloat16),
            pltpu.VMEM((2, beam_count, rows, length), jnp.bfloat16),
            pltpu.VMEM((beam_count - 1, 2, rows, length), jnp.bfloat16),
            pltpu.SemaphoreType.DMA((comp_count - 1, CHUNKS)),
            pltpu.SemaphoreType.DMA((comp_count - 1, CHUNKS)),
            pltpu.SemaphoreType.DMA((beam_count - 1, CHUNKS)),
            pltpu.SemaphoreType.DMA((beam_count - 1, CHUNKS)),
        ],
        compiler_params=pltpu.CompilerParams(
            collective_id=0, has_side_effects=True, vmem_limit_bytes=56 * 2**20
        ),
    )(part)


def band_matrix(offset, weight, span):
    tap_index = offset[:, None] + BAND // 2 + jnp.arange(BAND, dtype=jnp.int32)[None, :]
    matches = tap_index[:, :, None] == jnp.arange(span, dtype=jnp.int32)[None, None, :]
    return jnp.sum(
        jnp.where(matches, weight[:, :, None], jnp.zeros_like(weight)[:, :, None]), axis=1
    )


def exchange_kernel(
    counts, spread, image_ref, out_ref, send_sem, recv_sem, low_send, low_recv, high_send,
    high_recv, own_sem,
):
    sub_count, beam_count, comp_count = counts
    s = lax.axis_index("sub")
    block = lax.axis_index("beam") * comp_count + lax.axis_index("comp")
    has_low = block > 0
    has_high = block < beam_count * comp_count - 1
    width = out_ref.shape[-1]
    hops = sub_count if spread else 1

    def place(d, step):
        target = block + step
        return {
            "sub": lax.rem(s + d, sub_count),
            "beam": lax.div(target, comp_count),
            "comp": lax.rem(target, comp_count),
        }

    def columns(d):
        if not spread:
            return pl.ds(0, width)
        return pl.ds(pl.multiple_of(lax.rem(s + d, sub_count) * width, 128), width)

    barrier = pltpu.get_barrier_semaphore()
    for d in range(1, hops):
        pl.semaphore_signal(barrier, inc=1, device_id=place(d, 0), device_id_type=MESH)

    @pl.when(has_high)
    def _():
        for d in range(hops):
            pl.semaphore_signal(barrier, inc=1, device_id=place(d, 1), device_id_type=MESH)

    @pl.when(has_low)
    def _():
        for d in range(hops):
            pl.semaphore_signal(barrier, inc=1, device_id=place(d, -1), device_id_type=MESH)

    amount = hops - 1 + hops * (has_low.astype(jnp.int32) + has_high.astype(jnp.int32))
    pl.semaphore_wait(barrier, amount)

    def halo(d, step):
        source = slice(None) if not spread else s
        half = 1 if step > 0 else 0
        slot = 0 if step > 0 else out_ref.shape[2] - 1
        target = out_ref.at[:, :, slot] if not spread else out_ref.at[source, :, slot]
        origin = (
            image_ref.at[:, :, half]
            if not spread
            else image_ref.at[:, half, :, columns(d)]
        )
        return pltpu.make_async_remote_copy(
            src_ref=origin,
            dst_ref=target,
            send_sem=(low_send if step > 0 else high_send).at[d],
            recv_sem=(low_recv if step > 0 else high_recv).at[d],
            device_id=place(d, step),
            device_id_type=MESH,
        )

    @pl.when(has_high)
    def _():
        for d in range(hops):
            halo(d, 1).start()

    @pl.when(has_low)
    def _():
        for d in range(hops):
            halo(d, -1).start()

    copies = []
    for d in range(1, hops):
        copy = pltpu.make_async_remote_copy(
            src_ref=image_ref.at[:, :, :, columns(d)],
            dst_ref=out_ref.at[s, :, pl.ds(1, 2)],
            send_sem=send_sem.at[d],
            recv_sem=recv_sem.at[d],
            device_id=place(d, 0),
            device_id_type=MESH,
        )
        copy.start()
        copies.append(copy)
    if spread:
        own = pltpu.make_async_copy(
            image_ref.at[:, :, :, columns(0)], out_ref.at[s, :, pl.ds(1, 2)], own_sem
        )
        own.start()
        copies.append(own)

    low_slot = 0
    high_slot = out_ref.shape[2] - 1
    blank = jnp.zeros(out_ref.shape[:2] + out_ref.shape[3:], out_ref.dtype)

    @pl.when(has_low)
    def _():
        for d in range(hops):
            halo(d, 1).wait_recv()
            halo(d, -1).wait_send()

    @pl.when(jnp.logical_not(has_low))
    def _():
        out_ref[:, :, low_slot] = blank

    @pl.when(has_high)
    def _():
        for d in range(hops):
            halo(d, -1).wait_recv()
            halo(d, 1).wait_send()

    @pl.when(jnp.logical_not(has_high))
    def _():
        out_ref[:, :, high_slot] = blank

    for copy in copies:
        copy.wait()


def exchange(image, shape, counts, spread, kernel_id):
    hops = counts[0] if spread else 1
    return pl.pallas_call(
        functools.partial(exchange_kernel, counts, spread),
        out_shape=jax.ShapeDtypeStruct(shape, jnp.bfloat16),
        in_specs=[pl.BlockSpec(memory_space=pltpu.VMEM)],
        out_specs=pl.BlockSpec(memory_space=pltpu.VMEM),
        scratch_shapes=[pltpu.SemaphoreType.DMA((hops,))] * 6 + [pltpu.SemaphoreType.DMA],
        compiler_params=pltpu.CompilerParams(
            collective_id=kernel_id, has_side_effects=True, vmem_limit_bytes=24 * 2**20
        ),
    )(image)


def phases(delay, start, width):
    coarse_row = (start + RADIX * jnp.arange(width // RADIX, dtype=jnp.int32)).astype(jnp.float32)
    coarse = delay[..., None] * (1.0 + coarse_row / NR)
    fine = delay[..., None] * (jnp.arange(RADIX, dtype=jnp.float32) / NR)
    cos_one, sin_one = jnp.cos(coarse)[..., None], jnp.sin(coarse)[..., None]
    cos_two, sin_two = jnp.cos(fine)[..., None, :], jnp.sin(fine)[..., None, :]
    cosine = cos_one * cos_two - sin_one * sin_two
    sine = sin_one * cos_two + cos_one * sin_two
    shape = delay.shape + (width,)
    return cosine.reshape(shape), sine.reshape(shape)


def merge(window, offset, weight, cosine, sine):
    groups, span, width = window.shape[0] // 2, window.shape[2], window.shape[3]
    paired = window.reshape(groups, 2, 2, span, width)
    real_sum, imag_sum = 0.0, 0.0
    for c in range(2):
        matrix = band_matrix(offset[c], weight[c], span)
        high = matrix.astype(jnp.bfloat16)
        low = (matrix - high.astype(jnp.float32)).astype(jnp.bfloat16)
        both = jnp.concatenate([high, low], axis=0)
        blended = jnp.einsum(
            "jw,gpwr->gpjr", both, paired[:, c], preferred_element_type=jnp.float32
        )
        count = matrix.shape[0]
        blended = blended[:, :, :count] + blended[:, :, count:]
        real_sum += cosine[c] * blended[:, 0] - sine[c] * blended[:, 1]
        imag_sum += sine[c] * blended[:, 0] + cosine[c] * blended[:, 1]
    return real_sum, imag_sum


def body(raw_pulses, range_filter, steer_angle, band_offsets, band_weights, beam_delay):
    sub_count = lax.axis_size("sub")
    beam_devices = lax.axis_size("beam")
    comp_devices = lax.axis_size("comp")
    counts = (sub_count, beam_devices, comp_devices)
    blocks = beam_devices * comp_devices
    factor = float(raw_pulses.shape[0] * blocks) ** (-0.5)
    first_beams = steer_angle.shape[0] // blocks
    levels = sub_count.bit_length() - 1
    margin = BAND // 2
    width = NR // sub_count
    start = lax.axis_index("sub") * width
    cosine, sine = phases(beam_delay, start, width)
    weights = steering(steer_angle, factor)
    partial = beam_term(weights, raw_pulses).astype(jnp.bfloat16)
    summed = reduce_beams(partial, beam_devices, comp_devices)
    image = compress(summed, range_filter).astype(jnp.bfloat16)
    image = image.reshape(2, first_beams // margin, margin, NR)
    window = exchange(image, (sub_count, 2, 4, margin, width), counts, True, 1)
    window = window.reshape(sub_count, 2, 4 * margin, width)
    beam_count = first_beams
    for level_index in range(levels):
        base = first_beams * (2 ** (level_index + 1) - 2)
        cols = slice(base, base + 2 * beam_count)
        real, imag = merge(
            window, band_offsets[:, cols], band_weights[:, cols], cosine[:, cols], sine[:, cols]
        )
        beam_count *= 2
        if level_index + 1 < levels:
            image = jnp.stack([real, imag], 1).astype(jnp.bfloat16)
            groups = image.shape[0]
            ends = jnp.stack([image[:, :, :margin], image[:, :, -margin:]], 2)
            edges = exchange(
                ends, (groups, 2, 2, margin, width), counts, False, 2 + level_index
            )
            window = jnp.concatenate([edges[:, :, 0], image, edges[:, :, 1]], 2)
    return jnp.stack([real[0], imag[0]], 1)


def solution(mesh):
    in_specs = (
        P(("sub", "beam", "comp"), None, None),
        P(),
        P(None, ("sub", "beam", "comp")),
        P(None, ("beam", "comp")),
        P(None, ("beam", "comp"), None),
        P(None, ("beam", "comp")),
    )
    out_specs = P(("beam", "comp"), None, "sub")
    return jax.shard_map(body, mesh=mesh, in_specs=in_specs, out_specs=out_specs, check_vma=False)
```

```python
import functools
import math

import jax
import jax.numpy as jnp
from jax import lax
from jax.experimental import pallas as pl
from jax.experimental.pallas import tpu as pltpu
from jax.sharding import PartitionSpec as P

NR = 16384
RADIX = 128
BAND = 8
CHUNKS = 8
COMP_FIRST = 5
MESH = pl.DeviceIdType.MESH


def dft_table(length):
    index_row = jnp.arange(length, dtype=jnp.int32)
    product = index_row[:, None] * index_row[None, :] % length
    phase_angle = product.astype(jnp.float32) * (2.0 * math.pi / length)
    return (jnp.cos(phase_angle).astype(jnp.bfloat16), (-jnp.sin(phase_angle)).astype(jnp.bfloat16))


def real_form(length):
    cos_part, sin_part = dft_table(length)
    upper_rows = jnp.concatenate([cos_part, sin_part], axis=1)
    lower_rows = jnp.concatenate([-sin_part, cos_part], axis=1)
    return jnp.concatenate([upper_rows, lower_rows], axis=0)


def twiddle():
    freq_index = jnp.arange(RADIX, dtype=jnp.int32)[:, None]
    time_index = jnp.arange(RADIX, dtype=jnp.int32)[None, :]
    phase_angle = (freq_index * time_index % NR).astype(jnp.float32) * (2.0 * math.pi / NR)
    return (jnp.cos(phase_angle), -jnp.sin(phase_angle))


def compress(beams, range_filter):
    number = beams.shape[1]
    samples = beams.reshape(2, number, RADIX, RADIX)
    first = real_form(RADIX).reshape(2, RADIX, 2, RADIX)
    section_one = jnp.einsum("rpan,rask->spkn", samples, first, preferred_element_type=jnp.float32)
    cos_part, sin_part = twiddle()
    real_in = section_one[0]
    imag_in = section_one[1]
    turned = jnp.stack(
        [real_in * cos_part - imag_in * sin_part, real_in * sin_part + imag_in * cos_part], 0
    )
    high = turned.astype(jnp.bfloat16)
    low = (turned - high.astype(jnp.float32)).astype(jnp.bfloat16)
    spectrum = jnp.einsum("rpkn,rnsm->spmk", high, first, preferred_element_type=jnp.float32)
    spectrum += jnp.einsum("rpkn,rnsm->spmk", low, first, preferred_element_type=jnp.float32)
    spectrum = spectrum.reshape(2, number, NR)
    factor = NR ** (-0.5)
    real_out = (spectrum[0] * range_filter[0] - spectrum[1] * range_filter[1]) * factor
    imag_out = (spectrum[0] * range_filter[1] + spectrum[1] * range_filter[0]) * factor
    return jnp.stack([real_out, imag_out], 0)


def steering(phase_angle, factor):
    real_part = (jnp.cos(phase_angle) * factor).astype(jnp.bfloat16)
    imag_part = (jnp.sin(phase_angle) * factor).astype(jnp.bfloat16)
    upper_rows = jnp.stack([real_part, -imag_part], -1).reshape(phase_angle.shape[0], -1)
    lower_rows = jnp.stack([imag_part, real_part], -1).reshape(phase_angle.shape[0], -1)
    return jnp.concatenate([upper_rows, lower_rows], 0)


def reduce_kernel(
    beam_count, comp_count, comp_chunks, weight_ref, raw_ref, out_ref, raw, part, recv_one,
    send_two, recv_two, load_sem, one_send, one_recv, two_send, two_recv,
):
    sizes = {"beam": beam_count, "comp": comp_count}
    mine = {"beam": lax.axis_index("beam"), "comp": lax.axis_index("comp")}
    rows = out_ref.shape[1]
    width = raw_ref.shape[-1] // CHUNKS
    loads = []
    for j in range(CHUNKS):
        cols = pl.ds(j * width, width)
        loads.append(
            pltpu.make_async_copy(raw_ref.at[:, :, cols], raw.at[:, :, cols], load_sem.at[j])
        )
        loads[j].start()

    def peer_of(axis, d):
        return lax.rem(mine[axis] + d, sizes[axis])

    def route(j):
        beams_before = j * (CHUNKS - comp_chunks) // CHUNKS
        beams_after = (j + 1) * (CHUNKS - comp_chunks) // CHUNKS
        return ("beam", "comp") if beams_after > beams_before else ("comp", "beam")

    def owned(ref, axis, index, cols):
        if axis == "comp":
            return ref[:, :, index, :, cols]
        return ref[:, index, :, :, cols]

    barrier = pltpu.get_barrier_semaphore()
    for axis in sizes:
        for d in range(1, sizes[axis]):
            pl.semaphore_signal(
                barrier, inc=1, device_id={axis: peer_of(axis, d)}, device_id_type=MESH
            )
    pl.semaphore_wait(barrier, comp_count + beam_count - 2)
    first = []
    for j in range(CHUNKS):
        cols = pl.ds(j * width, width)
        loads[j].wait()
        pulses = raw[:, :, cols].reshape(-1, width)
        product = jnp.dot(weight_ref[...], pulses, preferred_element_type=jnp.float32)
        part[:, :, :, :, cols] = product.astype(jnp.bfloat16).reshape(
            2, beam_count, comp_count, rows, width
        )
        axis, other = route(j)
        group = []
        for d in range(1, sizes[axis]):
            peer = peer_of(axis, d)
            source = (
                part.at[:, :, peer, :, cols] if axis == "comp" else part.at[:, peer, :, :, cols]
            )
            copy = pltpu.make_async_remote_copy(
                src_ref=source,
                dst_ref=recv_one.at[d - 1, :, pl.ds(0, sizes[other]), :, cols],
                send_sem=one_send.at[d - 1, j],
                recv_sem=one_recv.at[d - 1, j],
                device_id={axis: peer},
                device_id_type=MESH,
            )
            copy.start()
            group.append(copy)
        first.append(group)
    second = []
    for j in range(CHUNKS):
        cols = pl.ds(j * width, width)
        axis, other = route(j)
        for copy in first[j]:
            copy.wait_recv()
        total = owned(part, axis, mine[axis], cols).astype(jnp.float32)
        for d in range(1, sizes[axis]):
            total += recv_one[d - 1, :, : sizes[other], :, cols].astype(jnp.float32)
        send_two[:, : sizes[other], :, cols] = total.astype(jnp.bfloat16)
        group = []
        for d in range(1, sizes[other]):
            peer = peer_of(other, d)
            copy = pltpu.make_async_remote_copy(
                src_ref=send_two.at[:, peer, :, cols],
                dst_ref=recv_two.at[d - 1, :, :, cols],
                send_sem=two_send.at[d - 1, j],
                recv_sem=two_recv.at[d - 1, j],
                device_id={other: peer},
                device_id_type=MESH,
            )
            copy.start()
            group.append(copy)
        second.append(group)
    for j in range(CHUNKS):
        cols = pl.ds(j * width, width)
        axis, other = route(j)
        for copy in second[j]:
            copy.wait_recv()
        total = part[:, mine["beam"], mine["comp"], :, cols].astype(jnp.float32)
        for d in range(1, sizes[axis]):
            total += recv_one[d - 1, :, mine[other], :, cols].astype(jnp.float32)
        for d in range(1, sizes[other]):
            total += recv_two[d - 1, :, :, cols].astype(jnp.float32)
        out_ref[:, :, cols] = total.astype(jnp.bfloat16)
    for group in first + second:
        for copy in group:
            copy.wait_send()


def reduce_beams(weights, raw_pulses, beam_count, comp_count):
    blocks = beam_count * comp_count
    rows = weights.shape[0] // (2 * blocks)
    length = raw_pulses.shape[2]
    most = max(beam_count, comp_count)
    return pl.pallas_call(
        functools.partial(reduce_kernel, beam_count, comp_count, COMP_FIRST),
        out_shape=jax.ShapeDtypeStruct((2, rows, length), jnp.bfloat16),
        in_specs=[
            pl.BlockSpec(memory_space=pltpu.VMEM),
            pl.BlockSpec(memory_space=pl.ANY),
        ],
        out_specs=pl.BlockSpec(memory_space=pltpu.VMEM),
        scratch_shapes=[
            pltpu.VMEM(raw_pulses.shape, jnp.bfloat16),
            pltpu.VMEM((2, beam_count, comp_count, rows, length), jnp.bfloat16),
            pltpu.VMEM((most - 1, 2, most, rows, length), jnp.bfloat16),
            pltpu.VMEM((2, most, rows, length), jnp.bfloat16),
            pltpu.VMEM((most - 1, 2, rows, length), jnp.bfloat16),
            pltpu.SemaphoreType.DMA((CHUNKS,)),
            pltpu.SemaphoreType.DMA((most - 1, CHUNKS)),
            pltpu.SemaphoreType.DMA((most - 1, CHUNKS)),
            pltpu.SemaphoreType.DMA((most - 1, CHUNKS)),
            pltpu.SemaphoreType.DMA((most - 1, CHUNKS)),
        ],
        compiler_params=pltpu.CompilerParams(
            collective_id=0, has_side_effects=True, vmem_limit_bytes=60 * 2**20
        ),
    )(weights, raw_pulses)


def band_matrix(offset, weight, span):
    tap_index = offset[:, None] + BAND // 2 + jnp.arange(BAND, dtype=jnp.int32)[None, :]
    matches = tap_index[:, :, None] == jnp.arange(span, dtype=jnp.int32)[None, None, :]
    return jnp.sum(
        jnp.where(matches, weight[:, :, None], jnp.zeros_like(weight)[:, :, None]), axis=1
    )


def exchange_kernel(
    counts, spread, image_ref, out_ref, send_sem, recv_sem, low_send, low_recv, high_send,
    high_recv, own_sem,
):
    sub_count, beam_count, comp_count = counts
    s = lax.axis_index("sub")
    block = lax.axis_index("beam") * comp_count + lax.axis_index("comp")
    has_low = block > 0
    has_high = block < beam_count * comp_count - 1
    width = out_ref.shape[-1]
    hops = sub_count if spread else 1

    def place(d, step):
        target = block + step
        return {
            "sub": lax.rem(s + d, sub_count),
            "beam": lax.div(target, comp_count),
            "comp": lax.rem(target, comp_count),
        }

    def columns(d):
        if not spread:
            return pl.ds(0, width)
        return pl.ds(pl.multiple_of(lax.rem(s + d, sub_count) * width, 128), width)

    barrier = pltpu.get_barrier_semaphore()
    for d in range(1, hops):
        pl.semaphore_signal(barrier, inc=1, device_id=place(d, 0), device_id_type=MESH)

    @pl.when(has_high)
    def _():
        for d in range(hops):
            pl.semaphore_signal(barrier, inc=1, device_id=place(d, 1), device_id_type=MESH)

    @pl.when(has_low)
    def _():
        for d in range(hops):
            pl.semaphore_signal(barrier, inc=1, device_id=place(d, -1), device_id_type=MESH)

    amount = hops - 1 + hops * (has_low.astype(jnp.int32) + has_high.astype(jnp.int32))
    pl.semaphore_wait(barrier, amount)

    def halo(d, step):
        source = slice(None) if not spread else s
        half = 1 if step > 0 else 0
        slot = 0 if step > 0 else out_ref.shape[2] - 1
        target = out_ref.at[:, :, slot] if not spread else out_ref.at[source, :, slot]
        origin = (
            image_ref.at[:, :, half]
            if not spread
            else image_ref.at[:, half, :, columns(d)]
        )
        return pltpu.make_async_remote_copy(
            src_ref=origin,
            dst_ref=target,
            send_sem=(low_send if step > 0 else high_send).at[d],
            recv_sem=(low_recv if step > 0 else high_recv).at[d],
            device_id=place(d, step),
            device_id_type=MESH,
        )

    @pl.when(has_high)
    def _():
        for d in range(hops):
            halo(d, 1).start()

    @pl.when(has_low)
    def _():
        for d in range(hops):
            halo(d, -1).start()

    copies = []
    for d in range(1, hops):
        copy = pltpu.make_async_remote_copy(
            src_ref=image_ref.at[:, :, :, columns(d)],
            dst_ref=out_ref.at[s, :, pl.ds(1, 2)],
            send_sem=send_sem.at[d],
            recv_sem=recv_sem.at[d],
            device_id=place(d, 0),
            device_id_type=MESH,
        )
        copy.start()
        copies.append(copy)
    if spread:
        own = pltpu.make_async_copy(
            image_ref.at[:, :, :, columns(0)], out_ref.at[s, :, pl.ds(1, 2)], own_sem
        )
        own.start()
        copies.append(own)

    low_slot = 0
    high_slot = out_ref.shape[2] - 1
    blank = jnp.zeros(out_ref.shape[:2] + out_ref.shape[3:], out_ref.dtype)

    @pl.when(has_low)
    def _():
        for d in range(hops):
            halo(d, 1).wait_recv()
            halo(d, -1).wait_send()

    @pl.when(jnp.logical_not(has_low))
    def _():
        out_ref[:, :, low_slot] = blank

    @pl.when(has_high)
    def _():
        for d in range(hops):
            halo(d, -1).wait_recv()
            halo(d, 1).wait_send()

    @pl.when(jnp.logical_not(has_high))
    def _():
        out_ref[:, :, high_slot] = blank

    for copy in copies:
        copy.wait()


def exchange(image, shape, counts, spread, kernel_id):
    hops = counts[0] if spread else 1
    return pl.pallas_call(
        functools.partial(exchange_kernel, counts, spread),
        out_shape=jax.ShapeDtypeStruct(shape, jnp.bfloat16),
        in_specs=[pl.BlockSpec(memory_space=pltpu.VMEM)],
        out_specs=pl.BlockSpec(memory_space=pltpu.VMEM),
        scratch_shapes=[pltpu.SemaphoreType.DMA((hops,))] * 6 + [pltpu.SemaphoreType.DMA],
        compiler_params=pltpu.CompilerParams(
            collective_id=kernel_id, has_side_effects=True, vmem_limit_bytes=24 * 2**20
        ),
    )(image)


def phases(delay, start, width):
    coarse_row = (start + RADIX * jnp.arange(width // RADIX, dtype=jnp.int32)).astype(jnp.float32)
    coarse = delay[..., None] * (1.0 + coarse_row / NR)
    fine = delay[..., None] * (jnp.arange(RADIX, dtype=jnp.float32) / NR)
    cos_one, sin_one = jnp.cos(coarse)[..., None], jnp.sin(coarse)[..., None]
    cos_two, sin_two = jnp.cos(fine)[..., None, :], jnp.sin(fine)[..., None, :]
    cosine = cos_one * cos_two - sin_one * sin_two
    sine = sin_one * cos_two + cos_one * sin_two
    shape = delay.shape + (width,)
    return cosine.reshape(shape), sine.reshape(shape)


def merge(window, offset, weight, cosine, sine):
    groups, span, width = window.shape[0] // 2, window.shape[2], window.shape[3]
    paired = window.reshape(groups, 2, 2, span, width)
    real_sum, imag_sum = 0.0, 0.0
    for c in range(2):
        matrix = band_matrix(offset[c], weight[c], span)
        high = matrix.astype(jnp.bfloat16)
        low = (matrix - high.astype(jnp.float32)).astype(jnp.bfloat16)
        both = jnp.concatenate([high, low], axis=0)
        blended = jnp.einsum(
            "jw,gpwr->gpjr", both, paired[:, c], preferred_element_type=jnp.float32
        )
        count = matrix.shape[0]
        blended = blended[:, :, :count] + blended[:, :, count:]
        real_sum += cosine[c] * blended[:, 0] - sine[c] * blended[:, 1]
        imag_sum += sine[c] * blended[:, 0] + cosine[c] * blended[:, 1]
    return real_sum, imag_sum


def body(raw_pulses, range_filter, steer_angle, band_offsets, band_weights, beam_delay):
    sub_count = lax.axis_size("sub")
    beam_devices = lax.axis_size("beam")
    comp_devices = lax.axis_size("comp")
    counts = (sub_count, beam_devices, comp_devices)
    blocks = beam_devices * comp_devices
    factor = float(raw_pulses.shape[0] * blocks) ** (-0.5)
    first_beams = steer_angle.shape[0] // blocks
    levels = sub_count.bit_length() - 1
    margin = BAND // 2
    width = NR // sub_count
    start = lax.axis_index("sub") * width
    cosine, sine = phases(beam_delay, start, width)
    weights = steering(steer_angle, factor)
    summed = reduce_beams(weights, raw_pulses, beam_devices, comp_devices)
    image = compress(summed, range_filter).astype(jnp.bfloat16)
    image = image.reshape(2, first_beams // margin, margin, NR)
    window = exchange(image, (sub_count, 2, 4, margin, width), counts, True, 1)
    window = window.reshape(sub_count, 2, 4 * margin, width)
    beam_count = first_beams
    for level_index in range(levels):
        base = first_beams * (2 ** (level_index + 1) - 2)
        cols = slice(base, base + 2 * beam_count)
        real, imag = merge(
            window, band_offsets[:, cols], band_weights[:, cols], cosine[:, cols], sine[:, cols]
        )
        beam_count *= 2
        if level_index + 1 < levels:
            image = jnp.stack([real, imag], 1).astype(jnp.bfloat16)
            groups = image.shape[0]
            ends = jnp.stack([image[:, :, :margin], image[:, :, -margin:]], 2)
            edges = exchange(
                ends, (groups, 2, 2, margin, width), counts, False, 2 + level_index
            )
            window = jnp.concatenate([edges[:, :, 0], image, edges[:, :, 1]], 2)
    return jnp.stack([real[0], imag[0]], 1)


def solution(mesh):
    in_specs = (
        P(("sub", "beam", "comp"), None, None),
        P(),
        P(None, ("sub", "beam", "comp")),
        P(None, ("beam", "comp")),
        P(None, ("beam", "comp"), None),
        P(None, ("beam", "comp")),
    )
    out_specs = P(("beam", "comp"), None, "sub")
    return jax.shard_map(body, mesh=mesh, in_specs=in_specs, out_specs=out_specs, check_vma=False)
```

```python
import functools
import math

import jax
import jax.numpy as jnp
from jax import lax
from jax.experimental import pallas as pl
from jax.experimental.pallas import tpu as pltpu
from jax.sharding import PartitionSpec as P

NR = 16384
RADIX = 128
BAND = 8
CHUNKS = 16
COMP_FIRST = CHUNKS
MESH = pl.DeviceIdType.MESH


def dft_table(length):
    index_row = jnp.arange(length, dtype=jnp.int32)
    product = index_row[:, None] * index_row[None, :] % length
    phase_angle = product.astype(jnp.float32) * (2.0 * math.pi / length)
    return (jnp.cos(phase_angle).astype(jnp.bfloat16), (-jnp.sin(phase_angle)).astype(jnp.bfloat16))


def real_form(length):
    cos_part, sin_part = dft_table(length)
    upper_rows = jnp.concatenate([cos_part, sin_part], axis=1)
    lower_rows = jnp.concatenate([-sin_part, cos_part], axis=1)
    return jnp.concatenate([upper_rows, lower_rows], axis=0)


def twiddle():
    freq_index = jnp.arange(RADIX, dtype=jnp.int32)[:, None]
    time_index = jnp.arange(RADIX, dtype=jnp.int32)[None, :]
    phase_angle = (freq_index * time_index % NR).astype(jnp.float32) * (2.0 * math.pi / NR)
    return (jnp.cos(phase_angle), -jnp.sin(phase_angle))


def compress(beams, range_filter):
    number = beams.shape[1]
    samples = beams.reshape(2, number, RADIX, RADIX)
    first = real_form(RADIX).reshape(2, RADIX, 2, RADIX)
    section_one = jnp.einsum("rpan,rask->spkn", samples, first, preferred_element_type=jnp.float32)
    cos_part, sin_part = twiddle()
    real_in = section_one[0]
    imag_in = section_one[1]
    turned = jnp.stack(
        [real_in * cos_part - imag_in * sin_part, real_in * sin_part + imag_in * cos_part], 0
    )
    high = turned.astype(jnp.bfloat16)
    low = (turned - high.astype(jnp.float32)).astype(jnp.bfloat16)
    spectrum = jnp.einsum("rpkn,rnsm->spmk", high, first, preferred_element_type=jnp.float32)
    spectrum += jnp.einsum("rpkn,rnsm->spmk", low, first, preferred_element_type=jnp.float32)
    spectrum = spectrum.reshape(2, number, NR)
    factor = NR ** (-0.5)
    real_out = (spectrum[0] * range_filter[0] - spectrum[1] * range_filter[1]) * factor
    imag_out = (spectrum[0] * range_filter[1] + spectrum[1] * range_filter[0]) * factor
    return jnp.stack([real_out, imag_out], 0)


def steering(phase_angle, factor):
    real_part = (jnp.cos(phase_angle) * factor).astype(jnp.bfloat16)
    imag_part = (jnp.sin(phase_angle) * factor).astype(jnp.bfloat16)
    upper_rows = jnp.stack([real_part, -imag_part], -1).reshape(phase_angle.shape[0], -1)
    lower_rows = jnp.stack([imag_part, real_part], -1).reshape(phase_angle.shape[0], -1)
    return jnp.concatenate([upper_rows, lower_rows], 0)


def reduce_kernel(
    beam_count, comp_count, comp_chunks, weight_ref, raw_ref, out_ref, raw, part, recv_one,
    send_two, recv_two, load_sem, one_send, one_recv, two_send, two_recv,
):
    sizes = {"beam": beam_count, "comp": comp_count}
    mine = {"beam": lax.axis_index("beam"), "comp": lax.axis_index("comp")}
    rows = out_ref.shape[1]
    width = raw_ref.shape[-1] // CHUNKS
    loads = []
    for j in range(CHUNKS):
        cols = pl.ds(j * width, width)
        loads.append(
            pltpu.make_async_copy(raw_ref.at[:, :, cols], raw.at[:, :, cols], load_sem.at[j])
        )
        loads[j].start()

    def peer_of(axis, d):
        return lax.rem(mine[axis] + d, sizes[axis])

    def route(j):
        beams_before = j * (CHUNKS - comp_chunks) // CHUNKS
        beams_after = (j + 1) * (CHUNKS - comp_chunks) // CHUNKS
        return ("beam", "comp") if beams_after > beams_before else ("comp", "beam")

    def owned(ref, axis, index, cols):
        if axis == "comp":
            return ref[:, :, index, :, cols]
        return ref[:, index, :, :, cols]

    barrier = pltpu.get_barrier_semaphore()
    for axis in sizes:
        for d in range(1, sizes[axis]):
            pl.semaphore_signal(
                barrier, inc=1, device_id={axis: peer_of(axis, d)}, device_id_type=MESH
            )
    pl.semaphore_wait(barrier, comp_count + beam_count - 2)
    first = []
    for j in range(CHUNKS):
        cols = pl.ds(j * width, width)
        loads[j].wait()
        pulses = raw[:, :, cols].reshape(-1, width)
        product = jnp.dot(weight_ref[...], pulses, preferred_element_type=jnp.float32)
        part[:, :, :, :, cols] = product.astype(jnp.bfloat16).reshape(
            2, beam_count, comp_count, rows, width
        )
        axis, other = route(j)
        group = []
        for d in range(1, sizes[axis]):
            peer = peer_of(axis, d)
            source = (
                part.at[:, :, peer, :, cols] if axis == "comp" else part.at[:, peer, :, :, cols]
            )
            copy = pltpu.make_async_remote_copy(
                src_ref=source,
                dst_ref=recv_one.at[d - 1, :, pl.ds(0, sizes[other]), :, cols],
                send_sem=one_send.at[d - 1, j],
                recv_sem=one_recv.at[d - 1, j],
                device_id={axis: peer},
                device_id_type=MESH,
            )
            copy.start()
            group.append(copy)
        first.append(group)
    second = []
    for j in range(CHUNKS):
        cols = pl.ds(j * width, width)
        axis, other = route(j)
        for copy in first[j]:
            copy.wait_recv()
        total = owned(part, axis, mine[axis], cols).astype(jnp.float32)
        for d in range(1, sizes[axis]):
            total += recv_one[d - 1, :, : sizes[other], :, cols].astype(jnp.float32)
        send_two[:, : sizes[other], :, cols] = total.astype(jnp.bfloat16)
        group = []
        for d in range(1, sizes[other]):
            peer = peer_of(other, d)
            copy = pltpu.make_async_remote_copy(
                src_ref=send_two.at[:, peer, :, cols],
                dst_ref=recv_two.at[d - 1, :, :, cols],
                send_sem=two_send.at[d - 1, j],
                recv_sem=two_recv.at[d - 1, j],
                device_id={other: peer},
                device_id_type=MESH,
            )
            copy.start()
            group.append(copy)
        second.append(group)
    for j in range(CHUNKS):
        cols = pl.ds(j * width, width)
        axis, other = route(j)
        for copy in second[j]:
            copy.wait_recv()
        total = part[:, mine["beam"], mine["comp"], :, cols].astype(jnp.float32)
        for d in range(1, sizes[axis]):
            total += recv_one[d - 1, :, mine[other], :, cols].astype(jnp.float32)
        for d in range(1, sizes[other]):
            total += recv_two[d - 1, :, :, cols].astype(jnp.float32)
        out_ref[:, :, cols] = total.astype(jnp.bfloat16)
    for group in first + second:
        for copy in group:
            copy.wait_send()


def reduce_beams(weights, raw_pulses, beam_count, comp_count):
    blocks = beam_count * comp_count
    rows = weights.shape[0] // (2 * blocks)
    length = raw_pulses.shape[2]
    most = max(beam_count, comp_count)
    return pl.pallas_call(
        functools.partial(reduce_kernel, beam_count, comp_count, COMP_FIRST),
        out_shape=jax.ShapeDtypeStruct((2, rows, length), jnp.bfloat16),
        in_specs=[
            pl.BlockSpec(memory_space=pltpu.VMEM),
            pl.BlockSpec(memory_space=pl.ANY),
        ],
        out_specs=pl.BlockSpec(memory_space=pltpu.VMEM),
        scratch_shapes=[
            pltpu.VMEM(raw_pulses.shape, jnp.bfloat16),
            pltpu.VMEM((2, beam_count, comp_count, rows, length), jnp.bfloat16),
            pltpu.VMEM((most - 1, 2, most, rows, length), jnp.bfloat16),
            pltpu.VMEM((2, most, rows, length), jnp.bfloat16),
            pltpu.VMEM((most - 1, 2, rows, length), jnp.bfloat16),
            pltpu.SemaphoreType.DMA((CHUNKS,)),
            pltpu.SemaphoreType.DMA((most - 1, CHUNKS)),
            pltpu.SemaphoreType.DMA((most - 1, CHUNKS)),
            pltpu.SemaphoreType.DMA((most - 1, CHUNKS)),
            pltpu.SemaphoreType.DMA((most - 1, CHUNKS)),
        ],
        compiler_params=pltpu.CompilerParams(
            collective_id=0, has_side_effects=True, vmem_limit_bytes=60 * 2**20
        ),
    )(weights, raw_pulses)


def band_matrix(offset, weight, span):
    tap_index = offset[:, None] + BAND // 2 + jnp.arange(BAND, dtype=jnp.int32)[None, :]
    matches = tap_index[:, :, None] == jnp.arange(span, dtype=jnp.int32)[None, None, :]
    return jnp.sum(
        jnp.where(matches, weight[:, :, None], jnp.zeros_like(weight)[:, :, None]), axis=1
    )


def exchange_kernel(
    counts, spread, image_ref, out_ref, send_sem, recv_sem, low_send, low_recv, high_send,
    high_recv, own_sem,
):
    sub_count, beam_count, comp_count = counts
    s = lax.axis_index("sub")
    block = lax.axis_index("beam") * comp_count + lax.axis_index("comp")
    has_low = block > 0
    has_high = block < beam_count * comp_count - 1
    width = out_ref.shape[-1]
    hops = sub_count if spread else 1

    def place(d, step):
        target = block + step
        return {
            "sub": lax.rem(s + d, sub_count),
            "beam": lax.div(target, comp_count),
            "comp": lax.rem(target, comp_count),
        }

    def columns(d):
        if not spread:
            return pl.ds(0, width)
        return pl.ds(pl.multiple_of(lax.rem(s + d, sub_count) * width, 128), width)

    barrier = pltpu.get_barrier_semaphore()
    for d in range(1, hops):
        pl.semaphore_signal(barrier, inc=1, device_id=place(d, 0), device_id_type=MESH)

    @pl.when(has_high)
    def _():
        for d in range(hops):
            pl.semaphore_signal(barrier, inc=1, device_id=place(d, 1), device_id_type=MESH)

    @pl.when(has_low)
    def _():
        for d in range(hops):
            pl.semaphore_signal(barrier, inc=1, device_id=place(d, -1), device_id_type=MESH)

    amount = hops - 1 + hops * (has_low.astype(jnp.int32) + has_high.astype(jnp.int32))
    pl.semaphore_wait(barrier, amount)

    def halo(d, step):
        source = slice(None) if not spread else s
        half = 1 if step > 0 else 0
        slot = 0 if step > 0 else out_ref.shape[2] - 1
        target = out_ref.at[:, :, slot] if not spread else out_ref.at[source, :, slot]
        origin = (
            image_ref.at[:, :, half]
            if not spread
            else image_ref.at[:, half, :, columns(d)]
        )
        return pltpu.make_async_remote_copy(
            src_ref=origin,
            dst_ref=target,
            send_sem=(low_send if step > 0 else high_send).at[d],
            recv_sem=(low_recv if step > 0 else high_recv).at[d],
            device_id=place(d, step),
            device_id_type=MESH,
        )

    @pl.when(has_high)
    def _():
        for d in range(hops):
            halo(d, 1).start()

    @pl.when(has_low)
    def _():
        for d in range(hops):
            halo(d, -1).start()

    copies = []
    for d in range(1, hops):
        copy = pltpu.make_async_remote_copy(
            src_ref=image_ref.at[:, :, :, columns(d)],
            dst_ref=out_ref.at[s, :, pl.ds(1, 2)],
            send_sem=send_sem.at[d],
            recv_sem=recv_sem.at[d],
            device_id=place(d, 0),
            device_id_type=MESH,
        )
        copy.start()
        copies.append(copy)
    if spread:
        own = pltpu.make_async_copy(
            image_ref.at[:, :, :, columns(0)], out_ref.at[s, :, pl.ds(1, 2)], own_sem
        )
        own.start()
        copies.append(own)

    low_slot = 0
    high_slot = out_ref.shape[2] - 1
    blank = jnp.zeros(out_ref.shape[:2] + out_ref.shape[3:], out_ref.dtype)

    @pl.when(has_low)
    def _():
        for d in range(hops):
            halo(d, 1).wait_recv()
            halo(d, -1).wait_send()

    @pl.when(jnp.logical_not(has_low))
    def _():
        out_ref[:, :, low_slot] = blank

    @pl.when(has_high)
    def _():
        for d in range(hops):
            halo(d, -1).wait_recv()
            halo(d, 1).wait_send()

    @pl.when(jnp.logical_not(has_high))
    def _():
        out_ref[:, :, high_slot] = blank

    for copy in copies:
        copy.wait()


def exchange(image, shape, counts, spread, kernel_id):
    hops = counts[0] if spread else 1
    return pl.pallas_call(
        functools.partial(exchange_kernel, counts, spread),
        out_shape=jax.ShapeDtypeStruct(shape, jnp.bfloat16),
        in_specs=[pl.BlockSpec(memory_space=pltpu.VMEM)],
        out_specs=pl.BlockSpec(memory_space=pltpu.VMEM),
        scratch_shapes=[pltpu.SemaphoreType.DMA((hops,))] * 6 + [pltpu.SemaphoreType.DMA],
        compiler_params=pltpu.CompilerParams(
            collective_id=kernel_id, has_side_effects=True, vmem_limit_bytes=24 * 2**20
        ),
    )(image)


def phases(delay, start, width):
    coarse_row = (start + RADIX * jnp.arange(width // RADIX, dtype=jnp.int32)).astype(jnp.float32)
    coarse = delay[..., None] * (1.0 + coarse_row / NR)
    fine = delay[..., None] * (jnp.arange(RADIX, dtype=jnp.float32) / NR)
    cos_one, sin_one = jnp.cos(coarse)[..., None], jnp.sin(coarse)[..., None]
    cos_two, sin_two = jnp.cos(fine)[..., None, :], jnp.sin(fine)[..., None, :]
    cosine = cos_one * cos_two - sin_one * sin_two
    sine = sin_one * cos_two + cos_one * sin_two
    shape = delay.shape + (width,)
    return cosine.reshape(shape), sine.reshape(shape)


def merge(window, offset, weight, cosine, sine):
    groups, span, width = window.shape[0] // 2, window.shape[2], window.shape[3]
    paired = window.reshape(groups, 2, 2, span, width)
    real_sum, imag_sum = 0.0, 0.0
    for c in range(2):
        matrix = band_matrix(offset[c], weight[c], span)
        high = matrix.astype(jnp.bfloat16)
        low = (matrix - high.astype(jnp.float32)).astype(jnp.bfloat16)
        both = jnp.concatenate([high, low], axis=0)
        blended = jnp.einsum(
            "jw,gpwr->gpjr", both, paired[:, c], preferred_element_type=jnp.float32
        )
        count = matrix.shape[0]
        blended = blended[:, :, :count] + blended[:, :, count:]
        real_sum += cosine[c] * blended[:, 0] - sine[c] * blended[:, 1]
        imag_sum += sine[c] * blended[:, 0] + cosine[c] * blended[:, 1]
    return real_sum, imag_sum


def body(raw_pulses, range_filter, steer_angle, band_offsets, band_weights, beam_delay):
    sub_count = lax.axis_size("sub")
    beam_devices = lax.axis_size("beam")
    comp_devices = lax.axis_size("comp")
    counts = (sub_count, beam_devices, comp_devices)
    blocks = beam_devices * comp_devices
    factor = float(raw_pulses.shape[0] * blocks) ** (-0.5)
    first_beams = steer_angle.shape[0] // blocks
    levels = sub_count.bit_length() - 1
    margin = BAND // 2
    width = NR // sub_count
    start = lax.axis_index("sub") * width
    cosine, sine = phases(beam_delay, start, width)
    weights = steering(steer_angle, factor)
    summed = reduce_beams(weights, raw_pulses, beam_devices, comp_devices)
    image = compress(summed, range_filter).astype(jnp.bfloat16)
    image = image.reshape(2, first_beams // margin, margin, NR)
    window = exchange(image, (sub_count, 2, 4, margin, width), counts, True, 1)
    window = window.reshape(sub_count, 2, 4 * margin, width)
    beam_count = first_beams
    for level_index in range(levels):
        base = first_beams * (2 ** (level_index + 1) - 2)
        cols = slice(base, base + 2 * beam_count)
        real, imag = merge(
            window, band_offsets[:, cols], band_weights[:, cols], cosine[:, cols], sine[:, cols]
        )
        beam_count *= 2
        if level_index + 1 < levels:
            image = jnp.stack([real, imag], 1).astype(jnp.bfloat16)
            groups = image.shape[0]
            ends = jnp.stack([image[:, :, :margin], image[:, :, -margin:]], 2)
            edges = exchange(
                ends, (groups, 2, 2, margin, width), counts, False, 2 + level_index
            )
            window = jnp.concatenate([edges[:, :, 0], image, edges[:, :, 1]], 2)
    return jnp.stack([real[0], imag[0]], 1)


def solution(mesh):
    in_specs = (
        P(("sub", "beam", "comp"), None, None),
        P(),
        P(None, ("sub", "beam", "comp")),
        P(None, ("beam", "comp")),
        P(None, ("beam", "comp"), None),
        P(None, ("beam", "comp")),
    )
    out_specs = P(("beam", "comp"), None, "sub")
    return jax.shard_map(body, mesh=mesh, in_specs=in_specs, out_specs=out_specs, check_vma=False)
```

```python
import functools
import math

import jax
import jax.numpy as jnp
from jax import lax
from jax.experimental import pallas as pl
from jax.experimental.pallas import tpu as pltpu
from jax.sharding import PartitionSpec as P

NR = 16384
RADIX = 128
BAND = 8
CHUNKS = 16
COMP_FIRST = CHUNKS
LAG = 3
MESH = pl.DeviceIdType.MESH


def dft_table(length):
    index_row = jnp.arange(length, dtype=jnp.int32)
    product = index_row[:, None] * index_row[None, :] % length
    phase_angle = product.astype(jnp.float32) * (2.0 * math.pi / length)
    return (jnp.cos(phase_angle).astype(jnp.bfloat16), (-jnp.sin(phase_angle)).astype(jnp.bfloat16))


def real_form(length):
    cos_part, sin_part = dft_table(length)
    upper_rows = jnp.concatenate([cos_part, sin_part], axis=1)
    lower_rows = jnp.concatenate([-sin_part, cos_part], axis=1)
    return jnp.concatenate([upper_rows, lower_rows], axis=0)


def twiddle():
    freq_index = jnp.arange(RADIX, dtype=jnp.int32)[:, None]
    time_index = jnp.arange(RADIX, dtype=jnp.int32)[None, :]
    phase_angle = (freq_index * time_index % NR).astype(jnp.float32) * (2.0 * math.pi / NR)
    return (jnp.cos(phase_angle), -jnp.sin(phase_angle))


def compress(beams, range_filter):
    number = beams.shape[1]
    samples = beams.reshape(2, number, RADIX, RADIX)
    first = real_form(RADIX).reshape(2, RADIX, 2, RADIX)
    section_one = jnp.einsum("rpan,rask->spkn", samples, first, preferred_element_type=jnp.float32)
    cos_part, sin_part = twiddle()
    real_in = section_one[0]
    imag_in = section_one[1]
    turned = jnp.stack(
        [real_in * cos_part - imag_in * sin_part, real_in * sin_part + imag_in * cos_part], 0
    )
    high = turned.astype(jnp.bfloat16)
    low = (turned - high.astype(jnp.float32)).astype(jnp.bfloat16)
    spectrum = jnp.einsum("rpkn,rnsm->spmk", high, first, preferred_element_type=jnp.float32)
    spectrum += jnp.einsum("rpkn,rnsm->spmk", low, first, preferred_element_type=jnp.float32)
    spectrum = spectrum.reshape(2, number, NR)
    factor = NR ** (-0.5)
    real_out = (spectrum[0] * range_filter[0] - spectrum[1] * range_filter[1]) * factor
    imag_out = (spectrum[0] * range_filter[1] + spectrum[1] * range_filter[0]) * factor
    return jnp.stack([real_out, imag_out], 0)


def steering(phase_angle, factor):
    real_part = (jnp.cos(phase_angle) * factor).astype(jnp.bfloat16)
    imag_part = (jnp.sin(phase_angle) * factor).astype(jnp.bfloat16)
    upper_rows = jnp.stack([real_part, -imag_part], -1).reshape(phase_angle.shape[0], -1)
    lower_rows = jnp.stack([imag_part, real_part], -1).reshape(phase_angle.shape[0], -1)
    return jnp.concatenate([upper_rows, lower_rows], 0)


def reduce_kernel(
    beam_count, comp_count, comp_chunks, weight_ref, raw_ref, out_ref, raw, part, recv_one,
    send_two, recv_two, load_sem, one_send, one_recv, two_send, two_recv,
):
    sizes = {"beam": beam_count, "comp": comp_count}
    mine = {"beam": lax.axis_index("beam"), "comp": lax.axis_index("comp")}
    rows = out_ref.shape[1]
    width = raw_ref.shape[-1] // CHUNKS
    loads = []
    for j in range(CHUNKS):
        cols = pl.ds(j * width, width)
        loads.append(
            pltpu.make_async_copy(raw_ref.at[:, :, cols], raw.at[:, :, cols], load_sem.at[j])
        )
        loads[j].start()

    def peer_of(axis, d):
        return lax.rem(mine[axis] + d, sizes[axis])

    def route(j):
        beams_before = j * (CHUNKS - comp_chunks) // CHUNKS
        beams_after = (j + 1) * (CHUNKS - comp_chunks) // CHUNKS
        return ("beam", "comp") if beams_after > beams_before else ("comp", "beam")

    def owned(ref, axis, index, cols):
        if axis == "comp":
            return ref[:, :, index, :, cols]
        return ref[:, index, :, :, cols]

    barrier = pltpu.get_barrier_semaphore()
    for axis in sizes:
        for d in range(1, sizes[axis]):
            pl.semaphore_signal(
                barrier, inc=1, device_id={axis: peer_of(axis, d)}, device_id_type=MESH
            )
    pl.semaphore_wait(barrier, comp_count + beam_count - 2)
    first = []
    second = []

    def start_first(j):
        cols = pl.ds(j * width, width)
        loads[j].wait()
        pulses = raw[:, :, cols].reshape(-1, width)
        product = jnp.dot(weight_ref[...], pulses, preferred_element_type=jnp.float32)
        part[:, :, :, :, cols] = product.astype(jnp.bfloat16).reshape(
            2, beam_count, comp_count, rows, width
        )
        axis, other = route(j)
        group = []
        for d in range(1, sizes[axis]):
            peer = peer_of(axis, d)
            source = (
                part.at[:, :, peer, :, cols] if axis == "comp" else part.at[:, peer, :, :, cols]
            )
            copy = pltpu.make_async_remote_copy(
                src_ref=source,
                dst_ref=recv_one.at[d - 1, :, pl.ds(0, sizes[other]), :, cols],
                send_sem=one_send.at[d - 1, j],
                recv_sem=one_recv.at[d - 1, j],
                device_id={axis: peer},
                device_id_type=MESH,
            )
            copy.start()
            group.append(copy)
        first.append(group)

    def start_second(j):
        cols = pl.ds(j * width, width)
        axis, other = route(j)
        for copy in first[j]:
            copy.wait_recv()
        total = owned(part, axis, mine[axis], cols).astype(jnp.float32)
        for d in range(1, sizes[axis]):
            total += recv_one[d - 1, :, : sizes[other], :, cols].astype(jnp.float32)
        send_two[:, : sizes[other], :, cols] = total.astype(jnp.bfloat16)
        group = []
        for d in range(1, sizes[other]):
            peer = peer_of(other, d)
            copy = pltpu.make_async_remote_copy(
                src_ref=send_two.at[:, peer, :, cols],
                dst_ref=recv_two.at[d - 1, :, :, cols],
                send_sem=two_send.at[d - 1, j],
                recv_sem=two_recv.at[d - 1, j],
                device_id={other: peer},
                device_id_type=MESH,
            )
            copy.start()
            group.append(copy)
        second.append(group)

    for j in range(CHUNKS + LAG):
        if j < CHUNKS:
            start_first(j)
        if j >= LAG:
            start_second(j - LAG)
    for j in range(CHUNKS):
        cols = pl.ds(j * width, width)
        axis, other = route(j)
        for copy in second[j]:
            copy.wait_recv()
        total = part[:, mine["beam"], mine["comp"], :, cols].astype(jnp.float32)
        for d in range(1, sizes[axis]):
            total += recv_one[d - 1, :, mine[other], :, cols].astype(jnp.float32)
        for d in range(1, sizes[other]):
            total += recv_two[d - 1, :, :, cols].astype(jnp.float32)
        out_ref[:, :, cols] = total.astype(jnp.bfloat16)
    for group in first + second:
        for copy in group:
            copy.wait_send()


def reduce_beams(weights, raw_pulses, beam_count, comp_count):
    blocks = beam_count * comp_count
    rows = weights.shape[0] // (2 * blocks)
    length = raw_pulses.shape[2]
    most = max(beam_count, comp_count)
    return pl.pallas_call(
        functools.partial(reduce_kernel, beam_count, comp_count, COMP_FIRST),
        out_shape=jax.ShapeDtypeStruct((2, rows, length), jnp.bfloat16),
        in_specs=[
            pl.BlockSpec(memory_space=pltpu.VMEM),
            pl.BlockSpec(memory_space=pl.ANY),
        ],
        out_specs=pl.BlockSpec(memory_space=pltpu.VMEM),
        scratch_shapes=[
            pltpu.VMEM(raw_pulses.shape, jnp.bfloat16),
            pltpu.VMEM((2, beam_count, comp_count, rows, length), jnp.bfloat16),
            pltpu.VMEM((most - 1, 2, most, rows, length), jnp.bfloat16),
            pltpu.VMEM((2, most, rows, length), jnp.bfloat16),
            pltpu.VMEM((most - 1, 2, rows, length), jnp.bfloat16),
            pltpu.SemaphoreType.DMA((CHUNKS,)),
            pltpu.SemaphoreType.DMA((most - 1, CHUNKS)),
            pltpu.SemaphoreType.DMA((most - 1, CHUNKS)),
            pltpu.SemaphoreType.DMA((most - 1, CHUNKS)),
            pltpu.SemaphoreType.DMA((most - 1, CHUNKS)),
        ],
        compiler_params=pltpu.CompilerParams(
            collective_id=0, has_side_effects=True, vmem_limit_bytes=60 * 2**20
        ),
    )(weights, raw_pulses)


def band_matrix(offset, weight, span):
    tap_index = offset[:, None] + BAND // 2 + jnp.arange(BAND, dtype=jnp.int32)[None, :]
    matches = tap_index[:, :, None] == jnp.arange(span, dtype=jnp.int32)[None, None, :]
    return jnp.sum(
        jnp.where(matches, weight[:, :, None], jnp.zeros_like(weight)[:, :, None]), axis=1
    )


def exchange_kernel(
    counts, spread, image_ref, out_ref, send_sem, recv_sem, low_send, low_recv, high_send,
    high_recv, own_sem,
):
    sub_count, beam_count, comp_count = counts
    s = lax.axis_index("sub")
    block = lax.axis_index("beam") * comp_count + lax.axis_index("comp")
    has_low = block > 0
    has_high = block < beam_count * comp_count - 1
    width = out_ref.shape[-1]
    hops = sub_count if spread else 1

    def place(d, step):
        target = block + step
        return {
            "sub": lax.rem(s + d, sub_count),
            "beam": lax.div(target, comp_count),
            "comp": lax.rem(target, comp_count),
        }

    def columns(d):
        if not spread:
            return pl.ds(0, width)
        return pl.ds(pl.multiple_of(lax.rem(s + d, sub_count) * width, 128), width)

    barrier = pltpu.get_barrier_semaphore()
    for d in range(1, hops):
        pl.semaphore_signal(barrier, inc=1, device_id=place(d, 0), device_id_type=MESH)

    @pl.when(has_high)
    def _():
        for d in range(hops):
            pl.semaphore_signal(barrier, inc=1, device_id=place(d, 1), device_id_type=MESH)

    @pl.when(has_low)
    def _():
        for d in range(hops):
            pl.semaphore_signal(barrier, inc=1, device_id=place(d, -1), device_id_type=MESH)

    amount = hops - 1 + hops * (has_low.astype(jnp.int32) + has_high.astype(jnp.int32))
    pl.semaphore_wait(barrier, amount)

    def halo(d, step):
        source = slice(None) if not spread else s
        half = 1 if step > 0 else 0
        slot = 0 if step > 0 else out_ref.shape[2] - 1
        target = out_ref.at[:, :, slot] if not spread else out_ref.at[source, :, slot]
        origin = (
            image_ref.at[:, :, half]
            if not spread
            else image_ref.at[:, half, :, columns(d)]
        )
        return pltpu.make_async_remote_copy(
            src_ref=origin,
            dst_ref=target,
            send_sem=(low_send if step > 0 else high_send).at[d],
            recv_sem=(low_recv if step > 0 else high_recv).at[d],
            device_id=place(d, step),
            device_id_type=MESH,
        )

    @pl.when(has_high)
    def _():
        for d in range(hops):
            halo(d, 1).start()

    @pl.when(has_low)
    def _():
        for d in range(hops):
            halo(d, -1).start()

    copies = []
    for d in range(1, hops):
        copy = pltpu.make_async_remote_copy(
            src_ref=image_ref.at[:, :, :, columns(d)],
            dst_ref=out_ref.at[s, :, pl.ds(1, 2)],
            send_sem=send_sem.at[d],
            recv_sem=recv_sem.at[d],
            device_id=place(d, 0),
            device_id_type=MESH,
        )
        copy.start()
        copies.append(copy)
    if spread:
        own = pltpu.make_async_copy(
            image_ref.at[:, :, :, columns(0)], out_ref.at[s, :, pl.ds(1, 2)], own_sem
        )
        own.start()
        copies.append(own)

    low_slot = 0
    high_slot = out_ref.shape[2] - 1
    blank = jnp.zeros(out_ref.shape[:2] + out_ref.shape[3:], out_ref.dtype)

    @pl.when(has_low)
    def _():
        for d in range(hops):
            halo(d, 1).wait_recv()
            halo(d, -1).wait_send()

    @pl.when(jnp.logical_not(has_low))
    def _():
        out_ref[:, :, low_slot] = blank

    @pl.when(has_high)
    def _():
        for d in range(hops):
            halo(d, -1).wait_recv()
            halo(d, 1).wait_send()

    @pl.when(jnp.logical_not(has_high))
    def _():
        out_ref[:, :, high_slot] = blank

    for copy in copies:
        copy.wait()


def exchange(image, shape, counts, spread, kernel_id):
    hops = counts[0] if spread else 1
    return pl.pallas_call(
        functools.partial(exchange_kernel, counts, spread),
        out_shape=jax.ShapeDtypeStruct(shape, jnp.bfloat16),
        in_specs=[pl.BlockSpec(memory_space=pltpu.VMEM)],
        out_specs=pl.BlockSpec(memory_space=pltpu.VMEM),
        scratch_shapes=[pltpu.SemaphoreType.DMA((hops,))] * 6 + [pltpu.SemaphoreType.DMA],
        compiler_params=pltpu.CompilerParams(
            collective_id=kernel_id, has_side_effects=True, vmem_limit_bytes=24 * 2**20
        ),
    )(image)


def phases(delay, start, width):
    coarse_row = (start + RADIX * jnp.arange(width // RADIX, dtype=jnp.int32)).astype(jnp.float32)
    coarse = delay[..., None] * (1.0 + coarse_row / NR)
    fine = delay[..., None] * (jnp.arange(RADIX, dtype=jnp.float32) / NR)
    cos_one, sin_one = jnp.cos(coarse)[..., None], jnp.sin(coarse)[..., None]
    cos_two, sin_two = jnp.cos(fine)[..., None, :], jnp.sin(fine)[..., None, :]
    cosine = cos_one * cos_two - sin_one * sin_two
    sine = sin_one * cos_two + cos_one * sin_two
    shape = delay.shape + (width,)
    return cosine.reshape(shape), sine.reshape(shape)


def merge(window, offset, weight, cosine, sine):
    groups, span, width = window.shape[0] // 2, window.shape[2], window.shape[3]
    paired = window.reshape(groups, 2, 2, span, width)
    real_sum, imag_sum = 0.0, 0.0
    for c in range(2):
        matrix = band_matrix(offset[c], weight[c], span)
        high = matrix.astype(jnp.bfloat16)
        low = (matrix - high.astype(jnp.float32)).astype(jnp.bfloat16)
        both = jnp.concatenate([high, low], axis=0)
        blended = jnp.einsum(
            "jw,gpwr->gpjr", both, paired[:, c], preferred_element_type=jnp.float32
        )
        count = matrix.shape[0]
        blended = blended[:, :, :count] + blended[:, :, count:]
        real_sum += cosine[c] * blended[:, 0] - sine[c] * blended[:, 1]
        imag_sum += sine[c] * blended[:, 0] + cosine[c] * blended[:, 1]
    return real_sum, imag_sum


def body(raw_pulses, range_filter, steer_angle, band_offsets, band_weights, beam_delay):
    sub_count = lax.axis_size("sub")
    beam_devices = lax.axis_size("beam")
    comp_devices = lax.axis_size("comp")
    counts = (sub_count, beam_devices, comp_devices)
    blocks = beam_devices * comp_devices
    factor = float(raw_pulses.shape[0] * blocks) ** (-0.5)
    first_beams = steer_angle.shape[0] // blocks
    levels = sub_count.bit_length() - 1
    margin = BAND // 2
    width = NR // sub_count
    start = lax.axis_index("sub") * width
    cosine, sine = phases(beam_delay, start, width)
    weights = steering(steer_angle, factor)
    summed = reduce_beams(weights, raw_pulses, beam_devices, comp_devices)
    image = compress(summed, range_filter).astype(jnp.bfloat16)
    image = image.reshape(2, first_beams // margin, margin, NR)
    window = exchange(image, (sub_count, 2, 4, margin, width), counts, True, 1)
    window = window.reshape(sub_count, 2, 4 * margin, width)
    beam_count = first_beams
    for level_index in range(levels):
        base = first_beams * (2 ** (level_index + 1) - 2)
        cols = slice(base, base + 2 * beam_count)
        real, imag = merge(
            window, band_offsets[:, cols], band_weights[:, cols], cosine[:, cols], sine[:, cols]
        )
        beam_count *= 2
        if level_index + 1 < levels:
            image = jnp.stack([real, imag], 1).astype(jnp.bfloat16)
            groups = image.shape[0]
            ends = jnp.stack([image[:, :, :margin], image[:, :, -margin:]], 2)
            edges = exchange(
                ends, (groups, 2, 2, margin, width), counts, False, 2 + level_index
            )
            window = jnp.concatenate([edges[:, :, 0], image, edges[:, :, 1]], 2)
    return jnp.stack([real[0], imag[0]], 1)


def solution(mesh):
    in_specs = (
        P(("sub", "beam", "comp"), None, None),
        P(),
        P(None, ("sub", "beam", "comp")),
        P(None, ("beam", "comp")),
        P(None, ("beam", "comp"), None),
        P(None, ("beam", "comp")),
    )
    out_specs = P(("beam", "comp"), None, "sub")
    return jax.shard_map(body, mesh=mesh, in_specs=in_specs, out_specs=out_specs, check_vma=False)
```
